768 devices in a mesh: gx: 32 (over x, y_hi, core), gy: 24 (over z, y_lo).
Axes of the slice: x: 4, y: 8 (y_hi: 4, y_lo: 2; y = y_hi * 2 + y_lo), z: 12, core: 2. Of those that a mesh axis runs over, the one named last changes fastest.
Arguments:
- fields: float32 [3, 8, 3072, 3072], P(None, None, 'gx', 'gy'), may hold values from -6 to 6
- terrain: int32 [3072, 3072], P('gx', 'gy'), may hold values from 0 to 2999
- parent_columns: bfloat16 [3, 60, 294912], P(None, None, ('gx', 'gy')), may hold values from -6 to 6
- record_tile: int32 [294912, 1], P(('gx', 'gy')), may hold values from 0 to 31; in each aligned block of 384 rows (0 to 383, 384 to 767, ...) at most 24 rows name the same one
- record_cells: int32 [294912, 4], P(('gx', 'gy')), may hold values from 0 to 191
- record_weights: bfloat16 [294912, 4], P(('gx', 'gy')), may hold values from 0.049804688 to 1
Outputs:
- updated_state: float32 [3, 8, 3072, 3072], P(None, None, 'gx', 'gy')
- nudge_coeffs: float32 [3, 8, 32, 32], replicated
The draws below stay inside these ranges and needn't reach their ends.
Inputs may be any that keep to these rules, and one draw needn't show every extreme that they name: `record_tile`: at most 24 of the 384 records of one device name the same tile index, and some device names one tile index exactly 24 times.
All inputs are finite; a program needn't handle non-finite values.
Results may differ from the reference program's by a relative error of at most 0.0003.
Values may be sent and summed in bfloat16 or wider, within the bound.
No kernel may reach another device: no remote copies, remote signals or barrier semaphores. Data moves between devices by JAX's collectives and lax.ppermute only.
A program may use at most 64 MiB of HBM per device.

```python
import math
import jax
import jax.numpy as jnp
import numpy as np
from jax import lax

LEV = 8
PREC = 384
NVAR = 3
PL = 60
KW = 32
KT = 4
RATIO = 8
NX = 3072
NY = 3072
NREC = 294912
TILE_COARSE_X = 12
TILE_COARSE_Y = 16
GC = 192
NXC = 384
NYC = 384
N_GX = 32
N_GY = 24


def set_ends(drawn, own_key, smallest, high):
    dims = drawn.shape
    spot = [jax.random.randint(jax.random.fold_in(own_key, axis), (), 0, dims[axis]) for axis in range(len(dims))]
    drawn = drawn.at[tuple(spot)].set(smallest)
    longest = dims.index(max(dims))
    spot[longest] = (spot[longest] + 1) % dims[longest]
    return drawn.at[tuple(spot)].set(high)


def steps_of(stream_key, extent, cuts, least, top_value):
    gain, own = 1.0, jax.random.fold_in(stream_key, 6)
    for position, blocks in cuts:
        draws = jnp.exp(jax.random.uniform(jax.random.fold_in(own, position), (blocks,), jnp.float32, least / len(cuts), top_value / len(cuts)))
        gain = gain * jnp.repeat(draws, extent[position] // blocks).reshape([-1 if axis == position else 1 for axis in range(len(extent))])
    return gain


def assign_block(key, own, number, rows, amount, top, reach, lean):
    order = jax.random.permutation(key, amount)
    heavy_load, common = shares(amount, rows * top, reach, lean, True), shares(amount, rows * top, reach, lean, False)
    places = jnp.arange(amount)

    def named(sizes, offset_by):
        used = int((sizes > 0).sum())
        fixed = max(1, used // 4)
        shifted = fixed + (places - fixed + offset_by * (used - fixed)) % max(1, amount - fixed)
        return jnp.zeros((amount,), jnp.int32).at[order[jnp.where(places < fixed, places, shifted)]].set(jnp.asarray(sizes, jnp.int32))

    sizes = jnp.where(number % 4 == 0, named(heavy_load, number // 4), named(common, number - number // 4 - 1))
    mixed = jax.random.permutation(jax.random.fold_in(own, 3), amount)
    source_of, sink = mixed[0:amount // 2 * 2:2], mixed[1:amount // 2 * 2:2]
    slack = jnp.minimum(sizes[source_of] - 1, reach - sizes[sink]) // 2
    slack = jnp.where((source_of == order[0]) | (sink == order[0]) | (sizes[sink] == 0), 0, jnp.maximum(slack, 0))
    shifted = jax.random.randint(jax.random.fold_in(own, 4), (amount // 2,), 0, 1 << 20) % (slack + 1)
    sizes = sizes.at[source_of].add(-shifted).at[sink].add(shifted)
    items = jnp.searchsorted(jnp.cumsum(sizes), jnp.arange(rows * top), side="right").astype(jnp.int32)
    grid = items.reshape(top, rows).T
    grid = grid[jax.random.permutation(jax.random.fold_in(own, 1), rows)]
    offset_by = jax.random.randint(jax.random.fold_in(own, 2), (rows, 1), 0, top)
    return jnp.take_along_axis(grid, (jnp.arange(top)[None, :] + offset_by) % top, axis=1)


def shares(number_of, total, limit, lean, full):
    weights = [(1 << 20) // math.isqrt(rank ** lean) + 1 for rank in range(1, number_of + 1)]
    largest = limit if full else min(limit, max(-(-total // number_of), total * weights[0] // sum(weights)))
    least = 1 if total - largest >= number_of - 1 else 0
    counts, rest = [largest] + [least] * (number_of - 1), total - largest - least * (number_of - 1)
    while rest > 0:
        candidates = [i for i in range(1, number_of) if counts[i] < largest] or [i for i in range(1, number_of) if counts[i] < limit]
        pool, left = sum([weights[i] for i in candidates]), rest
        for i in candidates:
            extra = min(limit - counts[i], max(1, left * weights[i] // pool), rest)
            counts[i] = counts[i] + extra
            rest = rest - extra
    return np.array(counts)


def centred(own_key, dims, scale, bound, shards=(), held_as=jnp.bfloat16):
    level = steps_of(own_key, dims, shards, -0.22, 0.18) if shards else 1.0
    drawn = jax.random.normal(own_key, dims, jnp.float32) * scale * level
    return jnp.minimum(jnp.maximum(drawn, -bound), bound).astype(held_as)


def setup_inputs(seed: int = 0) -> dict:
    keys = jax.random.split(jax.random.key(seed), 7)
    fields = centred(keys[0], (NVAR, LEV, NX, NY), 1.0, 6.0, ((2, 32), (3, 24)), jnp.float32)
    terrain = set_ends(jax.random.randint(keys[1], (NX, NY), 0, 3000), jax.random.fold_in(keys[1], 1), 0, 2999).astype(jnp.int32)
    parent_columns = centred(keys[2], (NVAR, PL, NREC), 1.0, 6.0, ((2, 768),))
    record_tile_keys = jax.random.split(jax.random.fold_in(keys[3], 1), NREC // PREC)
    record_tile_turns = jax.random.permutation(jax.random.fold_in(keys[3], 3), NREC // PREC)
    record_tile = jax.vmap(lambda own, number: assign_block(jax.random.fold_in(keys[3], 2), own, number, PREC, N_GX, 1, 2 * PREC // N_GX, 2))(record_tile_keys, record_tile_turns).reshape((NREC, 1))
    record_cells = set_ends(jax.random.randint(keys[4], (NREC, KT), 0, GC), jax.random.fold_in(keys[4], 1), 0, GC - 1).astype(jnp.int32)
    record_weights = jnp.clip(jnp.exp(math.log(1.0) - 2.9996462 * jax.random.uniform(keys[5], (NREC, KT), jnp.float32) ** steps_of(keys[5], (NREC, KT), ((0, 768),), -0.2, 0.2)), 0.049804688, 1.0).astype(jnp.bfloat16)
    return dict(fields=fields, terrain=terrain, parent_columns=parent_columns, record_tile=record_tile, record_cells=record_cells, record_weights=record_weights)


top_height = 12000.0

def octant_table():
    half_root = math.sqrt(0.5)
    cos_table = jnp.array([1.0, half_root, 0.0, -half_root, -1.0, -half_root, 0.0, half_root, 1.0], jnp.float32)
    sin_table = jnp.array([0.0, half_root, 1.0, half_root, 0.0, -half_root, -1.0, -half_root, 0.0], jnp.float32)
    return (cos_table, sin_table)

def wave_basis(positions, length, modes):
    half = modes // 2
    orders = jnp.arange(modes, dtype=jnp.int32)
    wave_number = jnp.where(orders < half, orders, orders - half + 1)
    phase_index = (wave_number[:, None] * positions[None, :] % length).astype(jnp.int32)
    octant = ((8 * phase_index + length // 2) // length).astype(jnp.int32)
    remainder = (8 * phase_index - octant * length).astype(jnp.int32)
    small_angle = 2.0 * math.pi / (8 * length) * remainder.astype(jnp.float32)
    cos_table, sin_table = octant_table()
    octant_hot = (octant[:, :, None] == jnp.arange(9, dtype=jnp.int32)[None, None, :]).astype(jnp.float32)
    cos_octant = lax.optimization_barrier(jnp.sum(octant_hot * cos_table, axis=2))
    sin_octant = lax.optimization_barrier(jnp.sum(octant_hot * sin_table, axis=2))
    cos_small = jnp.cos(small_angle)
    sin_small = jnp.sin(small_angle)
    cos_value = cos_octant * cos_small - sin_octant * sin_small
    sin_value = sin_octant * cos_small + cos_octant * sin_small
    wave_rows = jnp.where((orders < half)[:, None], cos_value, sin_value) * math.sqrt(2.0)
    return jnp.where((orders == 0)[:, None], jnp.ones_like(wave_rows), wave_rows)

def level_weights(heights, levels, parent_levels):
    spacing = (top_height - heights) / levels
    nest_height = heights[None, :] + (jnp.arange(levels, dtype=jnp.float32)[:, None] + 0.5) * spacing[None, :]
    parent_height = (jnp.arange(parent_levels, dtype=jnp.float32) + 0.5) * (top_height / parent_levels)
    hat_weights = jnp.maximum(0.0, 1.0 - jnp.abs(nest_height[:, None, :] - parent_height[None, :, None]) / spacing[None, None, :])
    return hat_weights / lax.optimization_barrier(jnp.sum(hat_weights, axis=1, keepdims=True))

def project(values, basis_x, basis_y):
    along_x = jnp.einsum('mx,vkxy->vkmy', basis_x, values, precision=lax.Precision.HIGHEST)
    return jnp.einsum('vkmy,ny->vkmn', along_x, basis_y, precision=lax.Precision.HIGHEST)

def expand(coeffs, basis_x, basis_y):
    along_y = jnp.einsum('vkmn,ny->vkmy', coeffs, basis_y, precision=lax.Precision.HIGHEST)
    return jnp.einsum('mx,vkmy->vkxy', basis_x, along_y, precision=lax.Precision.HIGHEST)

def advance(padded, values, wind_x, wind_y, inv_metric, low_modes):
    east_side = padded[:, :, 2:, 1:-1]
    west_side = padded[:, :, :-2, 1:-1]
    north_side = padded[:, :, 1:-1, 2:]
    south_side = padded[:, :, 1:-1, :-2]
    transport = 0.5 * (wind_x * (east_side - west_side) + wind_y * (north_side - south_side))
    diffusion = east_side + west_side + north_side + south_side - 4.0 * values
    level_above = jnp.concatenate([values[:, 1:], values[:, -1:]], axis=1)
    level_below = jnp.concatenate([values[:, :1], values[:, :-1]], axis=1)
    mixing = (level_above - 2.0 * values + level_below) * inv_metric
    return values - 0.1 * transport + 0.1 * diffusion + 0.1 * mixing - 4.0 * low_modes

def reference(fields, terrain, parent_columns, record_tile, record_cells, record_weights):
    record_ids = jnp.arange(NREC, dtype=jnp.int32)
    row_y = record_ids // PREC % N_GY
    target_position = record_tile[:, 0]
    columns = parent_columns.astype(jnp.float32)
    coarse = jnp.zeros((NVAR, PL, NXC * NYC), jnp.float32)
    for entry in range(KT):
        coarse_cell_index = record_cells[:, entry]
        first_coarse_cell = target_position * TILE_COARSE_X + coarse_cell_index // TILE_COARSE_Y
        coarse_b = row_y * TILE_COARSE_Y + coarse_cell_index % TILE_COARSE_Y
        flattened_index = (first_coarse_cell * NYC + coarse_b).astype(jnp.int32)
        weight_row = record_weights[:, entry].astype(jnp.float32)
        coarse = coarse.at[:, :, flattened_index].add(columns * weight_row[None, None, :])
    heights = terrain[::RATIO, ::RATIO].reshape(-1).astype(jnp.float32)
    vertical = level_weights(heights, LEV, PL)
    target = jnp.einsum('kpg,vpg->vkg', vertical, coarse, precision=lax.Precision.HIGHEST)
    target = target.reshape(NVAR, LEV, NXC, NYC)
    basis_x = wave_basis(jnp.arange(NX, dtype=jnp.int32), NX, KW)
    basis_y = wave_basis(jnp.arange(NY, dtype=jnp.int32), NY, KW)
    scale = 1.0 / math.sqrt(NX * NY)
    nest_part = project(fields, basis_x, basis_y) * scale
    target_part = project(target, basis_x[:, ::RATIO], basis_y[:, ::RATIO]) * (RATIO * RATIO * scale)
    nudge_coeffs = nest_part - target_part
    inv_metric = jnp.square(top_height / (top_height - terrain.astype(jnp.float32)))
    results = []
    for variable in range(NVAR):
        low_modes = expand(nudge_coeffs[variable:variable + 1], basis_x, basis_y) * scale
        single = fields[variable:variable + 1]
        padded = jnp.pad(single, ((0, 0), (0, 0), (1, 1), (1, 1)))
        results.append(advance(padded, single, fields[0:1], fields[1:2], inv_metric, low_modes))
    updated_state = jnp.concatenate(results, axis=0)
    return (updated_state, nudge_coeffs)
```

```python
import functools

import jax
import jax.numpy as jnp
import numpy as np
from jax import lax
from jax.experimental import pallas as pl
from jax.experimental.pallas import tpu as pltpu
from jax.sharding import PartitionSpec as P

KW = 32
RATIO = 8
TOP = 12000.0
LANES = 128
EXACT = lax.Precision.HIGHEST


def wave_rows(length):
    half = KW // 2
    x = np.arange(length)
    rows = [np.ones(length)]
    for m in range(1, half):
        rows.append(np.sqrt(2.0) * np.cos(2.0 * np.pi * (m * x % length) / length))
    for m in range(half, KW):
        rows.append(np.sqrt(2.0) * np.sin(2.0 * np.pi * ((m - half + 1) * x % length) / length))
    return np.stack(rows)


def two_parts(table):
    whole = table.astype(np.float32)
    high = whole.astype(jnp.bfloat16)
    low = (whole - high.astype(np.float32)).astype(jnp.bfloat16)
    return np.concatenate([high, low], axis=-2)


def dot(a, b, dims=((1,), (0,)), precision=None):
    return lax.dot_general(
        a, b, (dims, ((), ())), precision=precision, preferred_element_type=jnp.float32
    )


def rows_lanes(shape):
    return (
        lax.broadcasted_iota(jnp.int32, shape, 0),
        lax.broadcasted_iota(jnp.int32, shape, 1),
    )


def nest_kernel(here, f_ref, bx_ref, by_ref, p_ref, x0_ref, x1_ref, y0_ref, y1_ref):
    count, cells_x, cells_y = f_ref.shape
    per = LANES // KW
    row, lane = rows_lanes((cells_y, LANES))
    by4 = by_ref[0]
    spread = jnp.concatenate(
        [jnp.where(lane // KW == q, by4, 0.0) for q in range(per)], axis=0
    )
    bx = bx_ref[0]
    for g in range(count // per):
        values = jnp.concatenate([f_ref[per * g + q] for q in range(per)], axis=1)
        along_y = dot(values, spread, precision=EXACT)
        p_ref[:, pl.ds(g * LANES, LANES)] = dot(bx, along_y, precision=EXACT)
    row, lane = rows_lanes((cells_x, cells_y))
    for i in range(count):
        q = f_ref[i]
        x0_ref[i : i + 1, :] = q[0:1, :]
        x1_ref[i : i + 1, :] = q[cells_x - 1 : cells_x, :]
        for ref, at in ((y0_ref, 0), (y1_ref, cells_y - 1)):
            edge = jnp.broadcast_to(q[:, at : at + 1], q.shape)
            ref[i : i + 1, :] = jnp.sum(jnp.where(row == lane, edge, 0.0), axis=0, keepdims=True)


def record_kernel(
    here, h_ref, tile_ref, cells_ref, weights_ref, cols_ref, tabx_ref, taby_ref, p_ref, d_ref,
    col_ref, pick_ref, acc_ref, acc2_ref, *, levels, coarse_x, coarse_y, scale
):
    variables, parents, records = cols_ref.shape
    tiles = h_ref.shape[0]
    padded = h_ref.shape[1]
    coarse_all = tabx_ref.shape[1]
    for v in range(variables):
        col_ref[v] = cols_ref[v].astype(jnp.float32)
    tile = tile_ref[...]
    row, _ = rows_lanes((tiles, records))
    tile_hot = (row == tile).astype(jnp.float32).astype(jnp.bfloat16)
    heights = h_ref[...]
    high = jnp.floor(heights * (1.0 / 64.0))
    low = heights - 64.0 * high
    over = ((0,), (0,))
    pick_ref[...] = 64.0 * dot(high.astype(jnp.bfloat16), tile_hot, over) + dot(
        low.astype(jnp.bfloat16), tile_hot, over
    )
    acc_ref[...] = jnp.zeros_like(acc_ref)
    acc2_ref[...] = jnp.zeros_like(acc2_ref)
    row_c, _ = rows_lanes((padded, records))
    row_a, _ = rows_lanes((coarse_all, records))
    row_b, _ = rows_lanes((coarse_y, records))
    row_p, _ = rows_lanes((parents, records))
    parent = (row_p.astype(jnp.float32) + 0.5) * (TOP / parents)

    def entry(e, carry):
        cell = cells_ref[pl.ds(e, 1), :]
        weight = weights_ref[pl.ds(e, 1), :]
        height = jnp.sum(jnp.where(row_c == cell, pick_ref[...], 0.0), axis=0, keepdims=True)
        inner_x = cell // coarse_y
        a_hot = (row_a == tile * coarse_x + inner_x).astype(jnp.float32).astype(jnp.bfloat16)
        b_hot = (row_b == cell - inner_x * coarse_y).astype(jnp.float32).astype(jnp.bfloat16)
        bx2 = dot(tabx_ref[...], a_hot).astype(jnp.bfloat16)
        by2 = dot(taby_ref[0], b_hot)
        by = by2[:KW] + by2[KW:]
        spacing = (TOP - height) * (1.0 / levels)
        inverse = 1.0 / spacing
        apart = parent * inverse - (height * inverse + 0.5)
        uppers, lowers = [], []
        parts = [[None] * levels for _ in range(variables)]
        for k in range(levels):
            hat = jnp.maximum(0.0, 1.0 - jnp.abs(apart - float(k)))
            share = weight / jnp.sum(hat, axis=0, keepdims=True)
            for v in range(variables):
                parts[v][k] = jnp.sum(hat * col_ref[v], axis=0, keepdims=True) * share
        for v in range(variables):
            for k in range(levels):
                both = by * parts[v][k]
                upper = both.astype(jnp.bfloat16)
                uppers.append(upper)
                lowers.append((both - upper.astype(jnp.float32)).astype(jnp.bfloat16))
        last = ((1,), (1,))
        acc_ref[...] += dot(bx2, jnp.concatenate(uppers, axis=0), last)
        acc2_ref[...] += dot(bx2[:KW], jnp.concatenate(lowers, axis=0), last)
        return carry

    lax.fori_loop(0, cells_ref.shape[0], entry, 0)
    target = acc_ref[:KW] + acc_ref[KW:] + acc2_ref[...]
    d_ref[...] = p_ref[...] * scale - target * (RATIO * RATIO * scale)


def advance_kernel(
    here, f_ref, terrain_ref, n_ref, west_ref, east_ref, south_ref, north_ref, bx_ref, by_ref,
    out_ref, coeffs_ref, *, variables
):
    count, cells_x, cells_y = f_ref.shape
    levels = count // variables
    per = LANES // KW
    row, lane = rows_lanes((cells_x, cells_y))
    by4 = by_ref[0]
    block, _ = rows_lanes(by4.shape)
    nudge = n_ref[...]
    for i in range(count):
        coeffs_ref[i] = nudge[:, i * KW : (i + 1) * KW]
    along_x = dot(bx_ref[0], nudge, precision=EXACT)
    south = jnp.transpose(south_ref[...])
    north = jnp.transpose(north_ref[...])
    metric = TOP / (TOP - terrain_ref[...].astype(jnp.float32))
    metric = metric * metric * 0.1
    spreads = [jnp.where(block // KW == q, by4, 0.0) for q in range(per)]
    for i in range(count):
        k = i % levels
        q = f_ref[i]
        wind_x = f_ref[k]
        wind_y = f_ref[levels + k]
        east = jnp.where(row == cells_x - 1, east_ref[i : i + 1, :], pltpu.roll(q, cells_x - 1, 0))
        west = jnp.where(row == 0, west_ref[i : i + 1, :], pltpu.roll(q, 1, 0))
        above = jnp.where(lane == cells_y - 1, north[:cells_x, i : i + 1], pltpu.roll(q, cells_y - 1, 1))
        below = jnp.where(lane == 0, south[:cells_x, i : i + 1], pltpu.roll(q, 1, 1))
        transport = wind_x * (east - west) + wind_y * (above - below)
        diffusion = east + west + above + below - 4.0 * q
        upper = f_ref[i + 1] if k < levels - 1 else q
        lower = f_ref[i - 1] if k > 0 else q
        mixing = (upper - 2.0 * q + lower) * metric
        g = i // per
        low = dot(along_x[:, g * LANES : (g + 1) * LANES], spreads[i % per], precision=EXACT)
        out_ref[i] = q - 0.05 * transport + 0.1 * diffusion + mixing + low


def whole(shape):
    return pl.BlockSpec(shape, lambda i, here: (0,) * len(shape))


def picked(shape, which):
    return pl.BlockSpec((1,) + shape, lambda i, here: (here[which],) + (0,) * len(shape))


def call(kernel, here, ins, specs, outs, scratch=()):
    return pl.pallas_call(
        kernel,
        out_shape=[jax.ShapeDtypeStruct(s, jnp.float32) for s in outs],
        grid_spec=pltpu.PrefetchScalarGridSpec(
            num_scalar_prefetch=1,
            grid=(1,),
            in_specs=specs,
            out_specs=[whole(s) for s in outs],
            scratch_shapes=list(scratch),
        ),
        compiler_params=pltpu.CompilerParams(vmem_limit_bytes=48 << 20),
    )(here, *ins)


def gather(piece, axis):
    count = lax.axis_size(axis)
    return lax.all_to_all(
        jnp.broadcast_to(piece[None], (count,) + piece.shape), axis, 0, 0, tiled=True
    )


def shift(piece, axis, step):
    count = lax.axis_size(axis)
    return lax.ppermute(
        piece, axis, [(i, i + step) for i in range(count) if 0 <= i + step < count]
    )


def summed(part):
    count = lax.axis_size("gx")
    pieces = part.reshape(count, part.size // (count * LANES), LANES)
    mine = jnp.sum(lax.all_to_all(pieces, "gx", 0, 0, tiled=True), axis=0)
    mine = jnp.sum(gather(mine, "gy"), axis=0)
    return gather(mine, "gx").reshape(part.shape)


def per_device(fields, terrain, columns, record_tile, record_cells, record_weights):
    tiles_x, tiles_y = lax.axis_size("gx"), lax.axis_size("gy")
    variables, levels, cells_x, cells_y = fields.shape
    total_x, total_y = cells_x * tiles_x, cells_y * tiles_y
    coarse_x, coarse_y = cells_x // RATIO, cells_y // RATIO
    count = variables * levels
    wide = count * KW
    parents, records = columns.shape[1:]
    scale = 1.0 / np.sqrt(total_x * total_y)
    wave_x, wave_y = wave_rows(total_x), wave_rows(total_y)
    per = LANES // KW
    by_x = wave_x.reshape(KW, tiles_x, cells_x).transpose(1, 0, 2)
    by_y = wave_y.reshape(KW, tiles_y, cells_y).transpose(1, 0, 2)
    tab_bx = by_x.astype(np.float32)
    tab_bxt = (-4.0 * scale * by_x.transpose(0, 2, 1)).astype(np.float32)
    tab_by = np.tile(by_y, (1, per, 1)).astype(np.float32)
    tab_byt = np.tile(by_y.transpose(0, 2, 1), (1, 1, per)).astype(np.float32)
    tab_ax = two_parts(wave_x[:, ::RATIO])
    tab_ay = two_parts(by_y[:, :, ::RATIO])

    here = jnp.stack([lax.axis_index("gx"), lax.axis_index("gy")]).astype(jnp.int32)
    f = fields.reshape(count, cells_x, cells_y)

    coarse = coarse_x * coarse_y
    padded = -(-coarse // LANES) * LANES
    own = terrain[::RATIO, ::RATIO].astype(jnp.float32).reshape(coarse)
    own = jnp.pad(own, (0, padded - coarse)).reshape(padded // LANES, LANES)
    heights = gather(own, "gx").reshape(tiles_x, padded)

    nest, x0, x1, y0, y1 = call(
        nest_kernel,
        here,
        (f, tab_bx, tab_byt),
        [whole(f.shape), picked((KW, cells_x), 0), picked((cells_y, LANES), 1)],
        [(KW, wide)] + [(count, cells_y)] * 4,
    )
    west, east = shift(x1, "gx", 1), shift(x0, "gx", -1)
    south, north = shift(y1, "gy", 1), shift(y0, "gy", -1)

    flat = [record_tile.T, record_cells.T, record_weights.T.astype(jnp.float32)]
    (part,) = call(
        functools.partial(
            record_kernel, levels=levels, coarse_x=coarse_x, coarse_y=coarse_y, scale=scale
        ),
        here,
        (heights, *flat, columns, tab_ax, tab_ay, nest),
        [whole(heights.shape)]
        + [whole(x.shape) for x in flat]
        + [whole(columns.shape), whole(tab_ax.shape), picked(tab_ay.shape[1:], 1), whole(nest.shape)],
        [(KW, wide)],
        [
            pltpu.VMEM((variables, parents, records), jnp.float32),
            pltpu.VMEM((padded, records), jnp.float32),
            pltpu.VMEM((2 * KW, wide), jnp.float32),
            pltpu.VMEM((KW, wide), jnp.float32),
        ],
    )
    nudge = summed(part)

    updated, coeffs = call(
        functools.partial(advance_kernel, variables=variables),
        here,
        (f, terrain, nudge, west, east, south, north, tab_bxt, tab_by),
        [whole(x.shape) for x in (f, terrain, nudge, west, east, south, north)]
        + [picked((cells_x, KW), 0), picked((LANES, cells_y), 1)],
        [f.shape, (count, KW, KW)],
    )
    return updated.reshape(fields.shape), coeffs.reshape(variables, levels, KW, KW)


def solution(mesh):
    return jax.shard_map(
        per_device,
        mesh=mesh,
        in_specs=(
            P(None, None, "gx", "gy"),
            P("gx", "gy"),
            P(None, None, ("gx", "gy")),
            P(("gx", "gy"), None),
            P(("gx", "gy"), None),
            P(("gx", "gy"), None),
        ),
        out_specs=(P(None, None, "gx", "gy"), P()),
        check_vma=False,
    )
```

```python
import functools

import jax
import jax.numpy as jnp
import numpy as np
from jax import lax
from jax.experimental import pallas as pl
from jax.experimental.pallas import tpu as pltpu
from jax.sharding import PartitionSpec as P

KW = 32
RATIO = 8
TOP = 12000.0
LANES = 128
EXACT = lax.Precision.HIGHEST


def wave_rows(length):
    half = KW // 2
    x = np.arange(length)
    rows = [np.ones(length)]
    for m in range(1, half):
        rows.append(np.sqrt(2.0) * np.cos(2.0 * np.pi * (m * x % length) / length))
    for m in range(half, KW):
        rows.append(np.sqrt(2.0) * np.sin(2.0 * np.pi * ((m - half + 1) * x % length) / length))
    return np.stack(rows)


def two_parts(table, axis):
    whole = table.astype(np.float32)
    high = whole.astype(jnp.bfloat16)
    low = (whole - high.astype(np.float32)).astype(jnp.bfloat16)
    return np.concatenate([high, low], axis=axis)


def dot(a, b, dims=((1,), (0,)), precision=None):
    return lax.dot_general(
        a, b, (dims, ((), ())), precision=precision, preferred_element_type=jnp.float32
    )


def rows_lanes(shape):
    return (
        lax.broadcasted_iota(jnp.int32, shape, 0),
        lax.broadcasted_iota(jnp.int32, shape, 1),
    )


def split(x):
    high = x.astype(jnp.bfloat16)
    return high, (x - high.astype(jnp.float32)).astype(jnp.bfloat16)


def hot(mask):
    return jnp.where(mask, 1.0, 0.0).astype(jnp.bfloat16)


def ready_kernel(
    f_hbm, bx_hbm, by_hbm, tile_hbm, cells_hbm, tabx_hbm, p_ref, look_ref,
    f_ref, bx_ref, by_ref, tile_ref, cells_ref, tabx_ref, f_sem, bx_sem, by_sem, small_sem,
    *, coarse_x, coarse_y
):
    count, cells_x, cells_y = f_ref.shape
    per = LANES // KW
    groups = count // per
    fetch = [
        pltpu.make_async_copy(f_hbm.at[pl.ds(per * g, per)], f_ref.at[pl.ds(per * g, per)], f_sem.at[g])
        for g in range(groups)
    ]
    by_copy = pltpu.make_async_copy(by_hbm.at[lax.axis_index("gy")], by_ref, by_sem)
    bx_copy = pltpu.make_async_copy(bx_hbm.at[lax.axis_index("gx")], bx_ref, bx_sem)
    small = [
        pltpu.make_async_copy(a, b, small_sem.at[i])
        for i, (a, b) in enumerate(
            ((tile_hbm, tile_ref), (cells_hbm, cells_ref), (tabx_hbm, tabx_ref))
        )
    ]
    for copy in (*small, by_copy, *fetch, bx_copy):
        copy.start()
    for copy in small:
        copy.wait()
    records = tile_ref.shape[1]
    row_a, _ = rows_lanes((tabx_ref.shape[1], records))
    for e in range(cells_ref.shape[0]):
        where_x = tile_ref[...] * coarse_x + cells_ref[e : e + 1, :] // coarse_y
        look_ref[e] = dot(tabx_ref[...], hot(row_a == where_x)).astype(jnp.bfloat16)
    by_copy.wait()
    by4 = by_ref[...].astype(jnp.float32)
    _, lane = rows_lanes(by4.shape)
    spread = jnp.concatenate(
        [
            jnp.where(lane % LANES // KW == q, by4, 0.0).astype(jnp.bfloat16)
            for q in range(per)
        ],
        axis=0,
    )
    along = []
    for g in range(groups):
        fetch[g].wait()
        high, low = split(jnp.concatenate([f_ref[per * g + q] for q in range(per)], axis=1))
        both = dot(high, spread)
        along.append(both[:, :LANES] + both[:, LANES:] + dot(low, spread[:, :LANES]))
    high, low = split(jnp.concatenate(along, axis=1))
    bx_copy.wait()
    both = dot(bx_ref[...], high)
    p_ref[...] = both[:KW] + both[KW:] + dot(bx_ref[:KW, :], low)


def record_kernel(
    h_ref, tile_ref, cells_ref, weights_ref, cols_ref, look_ref, p_ref, taby_hbm, d_ref,
    col_ref, pick_ref, acc_ref, acc2_ref, taby_ref, sem, *, levels, coarse_y, scale
):
    variables, parents, records = cols_ref.shape
    tiles, padded = h_ref.shape
    fetch = pltpu.make_async_copy(taby_hbm.at[lax.axis_index("gy")], taby_ref, sem)
    fetch.start()
    tile = tile_ref[...]
    row, _ = rows_lanes((tiles, records))
    tile_hot = hot(row == tile)
    heights = h_ref[...]
    high = jnp.floor(heights * (1.0 / 64.0))
    low = heights - 64.0 * high
    over = ((0,), (0,))
    pick_ref[...] = 64.0 * dot(high.astype(jnp.bfloat16), tile_hot, over) + dot(
        low.astype(jnp.bfloat16), tile_hot, over
    )
    for v in range(variables):
        col_ref[v] = cols_ref[v].astype(jnp.float32)
    acc_ref[...] = jnp.zeros_like(acc_ref)
    acc2_ref[...] = jnp.zeros_like(acc2_ref)
    row_c, _ = rows_lanes((padded, records))
    row_b, _ = rows_lanes((coarse_y, records))
    row_p, _ = rows_lanes((parents, records))
    parent = (row_p.astype(jnp.float32) + 0.5) * (TOP / parents)
    last = ((1,), (1,))

    def entry(e, carry):
        cell = cells_ref[pl.ds(e, 1), :]
        weight = weights_ref[pl.ds(e, 1), :]
        height = jnp.sum(jnp.where(row_c == cell, pick_ref[...], 0.0), axis=0, keepdims=True)
        in_b = row_b == cell % coarse_y
        inverse = levels / (TOP - height)
        apart = parent * inverse - (height * inverse + 0.5)
        highs = [[None] * levels for _ in range(variables)]
        lows = [[None] * levels for _ in range(variables)]
        for k in range(levels):
            hat = jnp.maximum(0.0, 1.0 - jnp.abs(apart - float(k)))
            share = weight / jnp.sum(hat, axis=0, keepdims=True)
            for v in range(variables):
                value = jnp.sum(hat * col_ref[v], axis=0, keepdims=True) * share
                rest = value - value.astype(jnp.bfloat16).astype(jnp.float32)
                highs[v][k] = jnp.where(in_b, value, 0.0).astype(jnp.bfloat16)
                lows[v][k] = jnp.where(in_b, rest, 0.0).astype(jnp.bfloat16)
        look = look_ref[e]
        acc_ref[...] += dot(look, jnp.concatenate(sum(highs, []), axis=0), last)
        acc2_ref[...] += dot(look[:KW], jnp.concatenate(sum(lows, []), axis=0), last)
        return carry

    lax.fori_loop(0, cells_ref.shape[0], entry, 0)
    by_b = acc_ref[:KW] + acc_ref[KW:] + acc2_ref[...]
    some = LANES // coarse_y
    wide = some * KW
    groups = by_b.shape[1] // LANES
    fetch.wait()
    tall = jnp.concatenate([taby_ref[...]] * some, axis=0)
    row, lane = rows_lanes(tall.shape)
    tall = jnp.where(row // coarse_y == lane // KW, tall, 0.0)
    stacked = jnp.concatenate([by_b[:, g * LANES : (g + 1) * LANES] for g in range(groups)], axis=0)
    target = dot(stacked, tall, precision=EXACT)
    for g in range(groups):
        at = pl.ds(g * wide, wide)
        d_ref[:, at] = p_ref[:, at] * scale - target[g * KW : (g + 1) * KW] * (RATIO * RATIO * scale)


def edge_kernel(after, f_ref, *refs):
    outs, buffer, sem = refs[:4], refs[4], refs[5]
    count, cells_x, cells_y = f_ref.shape
    row, lane = rows_lanes((cells_x, cells_y))
    copies = [pltpu.make_async_copy(buffer.at[i], outs[i], sem.at[i]) for i in range(4)]
    for i in range(count):
        buffer[0, i : i + 1, :] = f_ref[i, 0:1, :]
        buffer[1, i : i + 1, :] = f_ref[i, cells_x - 1 : cells_x, :]
    copies[0].start()
    copies[1].start()
    for side, at in ((2, 0), (3, cells_y - 1)):
        for i in range(count):
            edge = jnp.broadcast_to(f_ref[i, :, at : at + 1], (cells_x, cells_y))
            buffer[side, i : i + 1, :] = jnp.sum(
                jnp.where(row == lane, edge, 0.0), axis=0, keepdims=True
            )
        copies[side].start()
    for copy in copies:
        copy.wait()


def stencil_kernel(
    after, f_ref, terrain_ref, west_ref, east_ref, south_ref, north_ref, out_ref, *, variables
):
    count, cells_x, cells_y = f_ref.shape
    levels = count // variables
    row, lane = rows_lanes((cells_x, cells_y))
    south = jnp.transpose(south_ref[...])
    north = jnp.transpose(north_ref[...])
    metric = TOP / (TOP - terrain_ref[...].astype(jnp.float32))
    metric = metric * metric * 0.1
    for i in range(count):
        k = i % levels
        q = f_ref[i]
        wind_x = f_ref[k]
        wind_y = f_ref[levels + k]
        east = jnp.where(row == cells_x - 1, east_ref[i : i + 1, :], pltpu.roll(q, cells_x - 1, 0))
        west = jnp.where(row == 0, west_ref[i : i + 1, :], pltpu.roll(q, 1, 0))
        above = jnp.where(
            lane == cells_y - 1, north[:cells_x, i : i + 1], pltpu.roll(q, cells_y - 1, 1)
        )
        below = jnp.where(lane == 0, south[:cells_x, i : i + 1], pltpu.roll(q, 1, 1))
        transport = wind_x * (east - west) + wind_y * (above - below)
        diffusion = east + west + above + below - 4.0 * q
        upper = f_ref[i + 1] if k < levels - 1 else q
        lower = f_ref[i - 1] if k > 0 else q
        mixing = (upper - 2.0 * q + lower) * metric
        out_ref[i] = q - 0.05 * transport + 0.1 * diffusion + mixing


def nudge_kernel(
    state_ref, n_ref, bx_hbm, by_hbm, out_hbm, coeffs_ref, out_ref, bx_ref, by_ref, low_ref,
    out_sem, bx_sem, by_sem
):
    count, cells_x, cells_y = state_ref.shape
    per = LANES // KW
    groups = count // per
    bx_copy = pltpu.make_async_copy(bx_hbm.at[lax.axis_index("gx")], bx_ref, bx_sem)
    by_copy = pltpu.make_async_copy(by_hbm.at[lax.axis_index("gy")], by_ref, by_sem)
    bx_copy.start()
    by_copy.start()
    nudge = n_ref[...]
    high, low = split(nudge)
    bx_copy.wait()
    along = dot(bx_ref[...], jnp.concatenate([high, high, low], axis=0))
    high, low = split(along)
    left = jnp.concatenate(
        [
            jnp.concatenate([x[:, g * LANES : (g + 1) * LANES] for x in (high, low, high)], axis=1)
            for g in range(groups)
        ],
        axis=0,
    )
    by_copy.wait()
    by4 = by_ref[...].astype(jnp.float32)
    block, _ = rows_lanes(by4.shape)
    right = jnp.concatenate(
        [jnp.where(block % LANES // KW == q, by4, 0.0).astype(jnp.bfloat16) for q in range(per)],
        axis=1,
    )
    low_ref[...] = dot(left, right)
    copies = []
    for g in range(groups):
        for q in range(per):
            i = per * g + q
            out_ref[i] = state_ref[i] + low_ref[
                g * cells_x : (g + 1) * cells_x, q * cells_y : (q + 1) * cells_y
            ]
        at = pl.ds(per * g, per)
        copies.append(pltpu.make_async_copy(out_ref.at[at], out_hbm.at[at], out_sem.at[g]))
        copies[-1].start()
    for i in range(count):
        coeffs_ref[i] = nudge[:, i * KW : (i + 1) * KW]
    for copy in copies:
        copy.wait()


FAR = pl.BlockSpec(memory_space=pltpu.HBM)
LOOSE = pl.BlockSpec(memory_space=pl.ANY)
NEAR = pl.BlockSpec(memory_space=pltpu.VMEM)
DMA = pltpu.SemaphoreType.DMA


def call(kernel, ins, specs, outs, out_specs, scratch=()):
    return pl.pallas_call(
        kernel,
        out_shape=[jax.ShapeDtypeStruct(s, d) for s, d in outs],
        in_specs=specs,
        out_specs=out_specs,
        scratch_shapes=list(scratch),
        compiler_params=pltpu.CompilerParams(vmem_limit_bytes=48 << 20),
    )(
        *[
            pltpu.with_memory_space_constraint(x, pltpu.HBM) if spec is FAR else x
            for x, spec in zip(ins, specs)
        ]
    )


def gather(piece, axis):
    count = lax.axis_size(axis)
    return lax.all_to_all(
        jnp.broadcast_to(piece[None], (count,) + piece.shape), axis, 0, 0, tiled=True
    )


def shift(piece, axis, step):
    count = lax.axis_size(axis)
    return lax.ppermute(
        piece, axis, [(i, i + step) for i in range(count) if 0 <= i + step < count]
    )


def per_device(fields, terrain, columns, record_tile, record_cells, record_weights):
    tiles_x, tiles_y = lax.axis_size("gx"), lax.axis_size("gy")
    variables, levels, cells_x, cells_y = fields.shape
    total_x, total_y = cells_x * tiles_x, cells_y * tiles_y
    coarse_x, coarse_y = cells_x // RATIO, cells_y // RATIO
    count = variables * levels
    wide = count * KW
    parents, records = columns.shape[1:]
    entries = record_cells.shape[1]
    scale = 1.0 / np.sqrt(total_x * total_y)
    per = LANES // KW
    f32, b16 = jnp.float32, jnp.bfloat16

    wave_x, wave_y = wave_rows(total_x), wave_rows(total_y)
    by_x = wave_x.reshape(KW, tiles_x, cells_x).transpose(1, 0, 2)
    by_y = wave_y.reshape(KW, tiles_y, cells_y).transpose(1, 0, 2)
    tab_bx = two_parts(by_x, -2)
    tab_byt = two_parts(np.tile(by_y.transpose(0, 2, 1), (1, 1, per)), -1)
    tab_ax = two_parts(wave_x[:, ::RATIO], -2)
    tab_ay = np.tile(
        by_y[:, :, ::RATIO].transpose(0, 2, 1), (1, 1, LANES // coarse_y)
    ).astype(np.float32)
    tab_low_x = two_parts(-4.0 * scale * by_x.transpose(0, 2, 1), -1)
    tab_low_x = np.concatenate([tab_low_x, tab_low_x[..., :KW]], axis=-1)
    tab_low_y = two_parts(np.tile(by_y, (1, per, 1)), -2)
    tab_low_y = np.concatenate(
        [tab_low_y[:, :LANES], tab_low_y[:, :LANES], tab_low_y[:, LANES:]], axis=1
    )

    f = fields.reshape(count, cells_x, cells_y)
    coarse = coarse_x * coarse_y
    padded = -(-coarse // LANES) * LANES
    own = terrain[::RATIO, ::RATIO].astype(f32).reshape(coarse)
    own = jnp.pad(own, (0, padded - coarse)).reshape(padded // LANES, LANES)
    heights = gather(own, "gx").reshape(tiles_x, padded)

    tile, cells = record_tile.T, record_cells.T
    nest, look = call(
        functools.partial(ready_kernel, coarse_x=coarse_x, coarse_y=coarse_y),
        (f, tab_bx, tab_byt, tile, cells, tab_ax),
        [FAR] * 6,
        [((KW, wide), f32), ((entries, 2 * KW, records), b16)],
        [NEAR, NEAR],
        [
            pltpu.VMEM(f.shape, f32),
            pltpu.VMEM(tab_bx.shape[1:], b16),
            pltpu.VMEM(tab_byt.shape[1:], b16),
            pltpu.VMEM(tile.shape, jnp.int32),
            pltpu.VMEM(cells.shape, jnp.int32),
            pltpu.VMEM(tab_ax.shape, b16),
            DMA((count // per,)),
            DMA,
            DMA,
            DMA((3,)),
        ],
    )
    (part,) = call(
        functools.partial(record_kernel, levels=levels, coarse_y=coarse_y, scale=scale),
        (heights, tile, cells, record_weights.T.astype(f32), columns, look, nest, tab_ay),
        [NEAR] * 7 + [FAR],
        [((KW, wide), f32)],
        [NEAR],
        [
            pltpu.VMEM(columns.shape, f32),
            pltpu.VMEM((padded, records), f32),
            pltpu.VMEM((2 * KW, count * coarse_y), f32),
            pltpu.VMEM((KW, count * coarse_y), f32),
            pltpu.VMEM(tab_ay.shape[1:], f32),
            DMA,
        ],
    )
    x0, x1, y0, y1 = call(
        edge_kernel,
        (part, f),
        [LOOSE, NEAR],
        [((count, cells_y), f32)] * 4,
        [FAR] * 4,
        [pltpu.VMEM((4, count, cells_y), f32), DMA((4,))],
    )

    pieces = part.reshape(tiles_x, part.size // (tiles_x * LANES), LANES)
    mine = jnp.sum(lax.all_to_all(pieces, "gx", 0, 0, tiled=True), axis=0)
    west, east = shift(x1, "gx", 1), shift(x0, "gx", -1)
    mine, west, east, y0, y1 = lax.optimization_barrier((mine, west, east, y0, y1))
    south, north = shift(y1, "gy", 1), shift(y0, "gy", -1)
    mine = jnp.sum(gather(mine, "gy"), axis=0)
    mine, south, north = lax.optimization_barrier((mine, south, north))
    nudge = gather(mine, "gx").reshape(part.shape)

    (state,) = call(
        functools.partial(stencil_kernel, variables=variables),
        (mine, f, terrain, west, east, south, north),
        [LOOSE] + [NEAR] * 6,
        [(f.shape, f32)],
        [NEAR],
    )
    updated, coeffs = call(
        nudge_kernel,
        (state, nudge, tab_low_x, tab_low_y),
        [NEAR, NEAR, FAR, FAR],
        [(f.shape, f32), ((count, KW, KW), f32)],
        [FAR, NEAR],
        [
            pltpu.VMEM(f.shape, f32),
            pltpu.VMEM(tab_low_x.shape[1:], b16),
            pltpu.VMEM(tab_low_y.shape[1:], b16),
            pltpu.VMEM((count // per * cells_x, per * cells_y), f32),
            DMA((count // per,)),
            DMA,
            DMA,
        ],
    )
    return updated.reshape(fields.shape), coeffs.reshape(variables, levels, KW, KW)


def solution(mesh):
    return jax.shard_map(
        per_device,
        mesh=mesh,
        in_specs=(
            P(None, None, "gx", "gy"),
            P("gx", "gy"),
            P(None, None, ("gx", "gy")),
            P(("gx", "gy"), None),
            P(("gx", "gy"), None),
            P(("gx", "gy"), None),
        ),
        out_specs=(P(None, None, "gx", "gy"), P()),
        check_vma=False,
    )
```

```python
import functools

import jax
import jax.numpy as jnp
import numpy as np
from jax import lax
from jax.experimental import pallas as pl
from jax.experimental.pallas import tpu as pltpu
from jax.sharding import PartitionSpec as P

KW = 32
RATIO = 8
TOP = 12000.0
HIGHEST_CELL = 2999.0
LANES = 128
EXACT = lax.Precision.HIGHEST


def wave_rows(length):
    half = KW // 2
    x = np.arange(length)
    rows = [np.ones(length)]
    for m in range(1, half):
        rows.append(np.sqrt(2.0) * np.cos(2.0 * np.pi * (m * x % length) / length))
    for m in range(half, KW):
        rows.append(np.sqrt(2.0) * np.sin(2.0 * np.pi * ((m - half + 1) * x % length) / length))
    return np.stack(rows)


def turns(outer, inner, length):
    half = KW // 2
    wave = np.arange(KW)
    wave = np.where(wave < half, wave, wave - half + 1)[:, None]
    a = 2.0 * np.pi * (wave * outer[None, :] % length) / length
    c = 2.0 * np.pi * (wave * inner[None, :] % length) / length
    size = np.where(wave == 0, 1.0, np.sqrt(2.0))
    cosine = np.arange(KW)[:, None] < half
    with_cos = size * np.where(cosine, np.cos(a), np.sin(a))
    with_sin = size * np.where(cosine, -np.sin(a), np.cos(a))
    return np.concatenate([with_cos, with_sin]), np.concatenate([np.cos(c), np.sin(c)])


def two_parts(table, axis):
    whole = table.astype(np.float32)
    high = whole.astype(jnp.bfloat16)
    low = (whole - high.astype(np.float32)).astype(jnp.bfloat16)
    return np.concatenate([high, low], axis=axis)


def dot(a, b, dims=((1,), (0,)), precision=None):
    return lax.dot_general(
        a, b, (dims, ((), ())), precision=precision, preferred_element_type=jnp.float32
    )


def rows_lanes(shape):
    return (
        lax.broadcasted_iota(jnp.int32, shape, 0),
        lax.broadcasted_iota(jnp.int32, shape, 1),
    )


def split(x):
    high = x.astype(jnp.bfloat16)
    return high, (x - high.astype(jnp.float32)).astype(jnp.bfloat16)


def by_parity(axis, a, b):
    first = lax.rem(lax.axis_index(axis), 2) == 0
    return jnp.where(first, a, b), jnp.where(first, b, a)


def hot(mask):
    return jnp.where(mask, 1.0, 0.0).astype(jnp.bfloat16)


def ready_kernel(
    f_hbm, bx_hbm, by_hbm, tile_hbm, cells_hbm, taba_hbm, tabc_hbm, p_ref, look_ref,
    xa_ref, xb_ref, ya_ref, yb_ref, f_ref, bx_ref, by_ref, tile_ref, cells_ref, taba_ref, tabc_ref, f_sem, bx_sem, by_sem, small_sem,
    *, coarse_y
):
    count, cells_x, cells_y = f_ref.shape
    per = LANES // KW
    groups = count // per
    fetch = pltpu.make_async_copy(f_hbm, f_ref, f_sem)
    by_copy = pltpu.make_async_copy(by_hbm.at[lax.axis_index("gy")], by_ref, by_sem)
    bx_copy = pltpu.make_async_copy(bx_hbm.at[lax.axis_index("gx")], bx_ref, bx_sem)
    small = [
        pltpu.make_async_copy(a, b, small_sem.at[i])
        for i, (a, b) in enumerate(
            (
                (tile_hbm, tile_ref),
                (cells_hbm, cells_ref),
                (taba_hbm, taba_ref),
                (tabc_hbm, tabc_ref),
            )
        )
    ]
    for copy in (*small, by_copy, fetch, bx_copy):
        copy.start()
    for copy in small:
        copy.wait()
    records = tile_ref.shape[1]
    row_t, _ = rows_lanes((taba_ref.shape[1], records))
    row_c, _ = rows_lanes((tabc_ref.shape[1], records))
    both = dot(taba_ref[...], hot(row_t == tile_ref[...]))
    outer = both[: 2 * KW] + both[2 * KW :]
    cells = cells_ref[...] // coarse_y
    for e in range(cells_ref.shape[0]):
        both = dot(tabc_ref[...], hot(row_c == cells[e : e + 1, :]))
        inner = both[: 2 * KW] + both[2 * KW :]
        turned = outer * inner
        high, low = split(turned[:KW] + turned[KW:])
        look_ref[:KW, e * records : (e + 1) * records] = high
        look_ref[KW:, e * records : (e + 1) * records] = low
    by_copy.wait()
    by4 = by_ref[...].astype(jnp.float32)
    _, lane = rows_lanes(by4.shape)
    spread = jnp.concatenate(
        [
            jnp.where(lane % LANES // KW == q, by4, 0.0).astype(jnp.bfloat16)
            for q in range(per)
        ],
        axis=0,
    )
    fetch.wait()
    bx_copy.wait()
    values = jnp.concatenate(
        [
            jnp.concatenate([f_ref[per * g + q] for q in range(per)], axis=1)
            for g in range(groups)
        ],
        axis=0,
    )
    high, low = split(values)
    both = dot(high, spread)
    along = both[:, :LANES] + both[:, LANES:] + dot(low, spread[:, :LANES])
    high, low = split(
        jnp.concatenate([along[g * cells_x : (g + 1) * cells_x] for g in range(groups)], axis=1)
    )
    both = dot(bx_ref[...], high)
    p_ref[...] = both[:KW] + both[KW:] + dot(bx_ref[:KW, :], low)
    row, lane = rows_lanes((cells_x, cells_y))
    for i in range(count):
        for ref, at in ((xa_ref, cells_x - 1), (xb_ref, 0)):
            ref[i : i + 1, :] = f_ref[i, at : at + 1, :]
        for ref, at in ((ya_ref, cells_y - 1), (yb_ref, 0)):
            edge = jnp.broadcast_to(f_ref[i, :, at : at + 1], (cells_x, cells_y))
            ref[i : i + 1, :] = jnp.sum(jnp.where(row == lane, edge, 0.0), axis=0, keepdims=True)
    for axis, a_ref, b_ref in (("gx", xa_ref, xb_ref), ("gy", ya_ref, yb_ref)):
        a_ref[...], b_ref[...] = by_parity(axis, a_ref[...], b_ref[...])


def reach(k, levels, parents, highest):
    bottoms = [h + (k - 0.5) * (TOP - h) / levels for h in (0.0, highest)]
    tops = [h + (k + 1.5) * (TOP - h) / levels for h in (0.0, highest)]
    step = TOP / parents
    first = int(np.floor((min(bottoms) - 1.0) / step - 0.5))
    last = int(np.ceil((max(tops) + 1.0) / step - 0.5)) + 1
    return max(0, first) // 8 * 8, min(-(-parents // 8), -(-last // 8)) * 8


def record_kernel(
    h_ref, tile_ref, cells_ref, weights_ref, cols_ref, look_ref, p_ref, taby_hbm, d_ref,
    col_ref, pick_ref, high_ref, low_ref, taby_ref, sem, *, levels, coarse_y, scale
):
    variables, parents, records = cols_ref.shape
    tiles, padded = h_ref.shape
    count = variables * levels
    fetch = pltpu.make_async_copy(taby_hbm.at[lax.axis_index("gy")], taby_ref, sem)
    fetch.start()
    tile = tile_ref[...]
    row, _ = rows_lanes((tiles, records))
    tile_hot = hot(row == tile)
    heights = h_ref[...]
    high = jnp.floor(heights * (1.0 / 64.0))
    low = heights - 64.0 * high
    over = ((0,), (0,))
    pick_ref[...] = 64.0 * dot(high.astype(jnp.bfloat16), tile_hot, over) + dot(
        low.astype(jnp.bfloat16), tile_hot, over
    )
    col_ref[...] = jnp.zeros_like(col_ref)
    for v in range(variables):
        col_ref[v, :parents, :] = cols_ref[v].astype(jnp.float32)
    row_c, _ = rows_lanes((padded, records))
    row_b, _ = rows_lanes((coarse_y, records))
    row_p, _ = rows_lanes(col_ref.shape[1:])
    parent = jnp.where(row_p < parents, (row_p.astype(jnp.float32) + 0.5) * (TOP / parents), 1e9)
    cells = cells_ref[...]
    weights = weights_ref[...].astype(jnp.float32)
    for e in range(cells_ref.shape[0]):
        at = slice(e * records, (e + 1) * records)
        cell = cells[e : e + 1, :]
        height = jnp.sum(jnp.where(row_c == cell, pick_ref[...], 0.0), axis=0, keepdims=True)
        in_b = row_b == cell % coarse_y
        inverse = levels / (TOP - height)
        shift_k = height * inverse + 0.5
        apart = parent * inverse - shift_k
        for k in range(levels):
            first, last = reach(k, levels, parents, HIGHEST_CELL)
            hat = jnp.maximum(0.0, 1.0 - jnp.abs(apart[first:last] - float(k)))
            share = weights[e : e + 1, :] / jnp.sum(hat, axis=0, keepdims=True)
            for v in range(variables):
                value = jnp.sum(hat * col_ref[v, first:last, :], axis=0, keepdims=True) * share
                rest = value - value.astype(jnp.bfloat16).astype(jnp.float32)
                i = (v * levels + k) * coarse_y
                high_ref[i : i + coarse_y, at] = jnp.where(in_b, value, 0.0).astype(jnp.bfloat16)
                low_ref[i : i + coarse_y, at] = jnp.where(in_b, rest, 0.0).astype(jnp.bfloat16)
    last = ((1,), (1,))
    both = dot(high_ref[...], look_ref[...], last)
    by_b = both[:, :KW] + both[:, KW:] + dot(low_ref[...], look_ref[:KW, :], last)
    some = LANES // coarse_y
    groups = count // some
    fetch.wait()
    tall = jnp.concatenate([taby_ref[...]] * some, axis=0)
    row, lane = rows_lanes(tall.shape)
    tall = jnp.where(row // coarse_y == lane // KW, tall, 0.0)
    for g in range(groups):
        target = dot(by_b[g * LANES : (g + 1) * LANES], tall, over, precision=EXACT)
        for i in range(some * KW // LANES):
            j = g * (some * KW // LANES) + i
            here = slice(j * LANES, (j + 1) * LANES)
            part = p_ref[:, here] * scale - target[:, i * LANES : (i + 1) * LANES] * (
                RATIO * RATIO * scale
            )
            for m in range(KW // 8):
                d_ref[:, m * p_ref.shape[1] // LANES + j, :] = part[8 * m : 8 * m + 8]


def stencil_kernel(
    after, f_ref, terrain_ref, xa_ref, xb_ref, ya_ref, yb_ref, out_ref, east_ref, west_ref,
    *, variables
):
    count, cells_x, cells_y = f_ref.shape
    levels = count // variables
    row, lane = rows_lanes((cells_x, cells_y))
    east_ref[...], west_ref[...] = by_parity("gx", xa_ref[...], xb_ref[...])
    north, south = by_parity("gy", ya_ref[...], yb_ref[...])
    south = jnp.transpose(south)
    north = jnp.transpose(north)
    metric = TOP / (TOP - terrain_ref[...].astype(jnp.float32))
    metric = metric * metric * 0.1
    for i in range(count):
        k = i % levels
        q = f_ref[i]
        wind_x = f_ref[k]
        wind_y = f_ref[levels + k]
        east = jnp.where(row == cells_x - 1, east_ref[i : i + 1, :], pltpu.roll(q, cells_x - 1, 0))
        west = jnp.where(row == 0, west_ref[i : i + 1, :], pltpu.roll(q, 1, 0))
        above = jnp.where(
            lane == cells_y - 1, north[:cells_x, i : i + 1], pltpu.roll(q, cells_y - 1, 1)
        )
        below = jnp.where(lane == 0, south[:cells_x, i : i + 1], pltpu.roll(q, 1, 1))
        transport = wind_x * (east - west) + wind_y * (above - below)
        diffusion = east + west + above + below - 4.0 * q
        upper = f_ref[i + 1] if k < levels - 1 else q
        lower = f_ref[i - 1] if k > 0 else q
        mixing = (upper - 2.0 * q + lower) * metric
        out_ref[i] = q - 0.05 * transport + 0.1 * diffusion + mixing


def nudge_kernel(
    state_ref, n_ref, bx_hbm, by_hbm, out_hbm, coeffs_hbm, out_ref, coeffs_ref, bx_ref, by_ref,
    low_ref, out_sem, coeffs_sem, bx_sem, by_sem
):
    count, cells_x, cells_y = state_ref.shape
    per = LANES // KW
    groups = count // per
    bx_copy = pltpu.make_async_copy(bx_hbm.at[lax.axis_index("gx")], bx_ref, bx_sem)
    by_copy = pltpu.make_async_copy(by_hbm.at[lax.axis_index("gy")], by_ref, by_sem)
    bx_copy.start()
    by_copy.start()
    nudge = jnp.concatenate(
        [
            jnp.concatenate([n_ref[:, m * groups + g, :] for m in range(KW // 8)], axis=0)
            for g in range(groups)
        ],
        axis=1,
    )
    high, low = split(nudge)
    bx_copy.wait()
    along = dot(bx_ref[...], jnp.concatenate([high, high, low], axis=0))
    high, low = split(along)
    by_copy.wait()
    by4 = by_ref[...].astype(jnp.float32)
    block, _ = rows_lanes(by4.shape)
    right = jnp.concatenate(
        [jnp.where(block % LANES // KW == q, by4, 0.0).astype(jnp.bfloat16) for q in range(per)],
        axis=1,
    )
    for i in range(count):
        coeffs_ref[i] = nudge[:, i * KW : (i + 1) * KW]
    copies = [pltpu.make_async_copy(coeffs_ref, coeffs_hbm, coeffs_sem)]
    copies[0].start()
    halves = 2
    some = groups // halves
    for half in range(halves):
        left = jnp.concatenate(
            [
                jnp.concatenate([x[:, g * LANES : (g + 1) * LANES] for x in (high, low, high)], axis=1)
                for g in range(half * some, (half + 1) * some)
            ],
            axis=0,
        )
        low_ref[...] = dot(left, right)
        for g in range(some):
            for q in range(per):
                i = per * (half * some + g) + q
                out_ref[i] = state_ref[i] + low_ref[
                    g * cells_x : (g + 1) * cells_x, q * cells_y : (q + 1) * cells_y
                ]
            at = pl.ds(per * (half * some + g), per)
            copies.append(
                pltpu.make_async_copy(out_ref.at[at], out_hbm.at[at], out_sem.at[half * some + g])
            )
            copies[-1].start()
    for copy in copies:
        copy.wait()


FAR = pl.BlockSpec(memory_space=pltpu.HBM)
LOOSE = pl.BlockSpec(memory_space=pl.ANY)
NEAR = pl.BlockSpec(memory_space=pltpu.VMEM)
DMA = pltpu.SemaphoreType.DMA


def call(kernel, ins, specs, outs, out_specs, scratch=()):
    return pl.pallas_call(
        kernel,
        out_shape=[jax.ShapeDtypeStruct(s, d) for s, d in outs],
        in_specs=specs,
        out_specs=out_specs,
        scratch_shapes=list(scratch),
        compiler_params=pltpu.CompilerParams(vmem_limit_bytes=48 << 20),
    )(
        *[
            pltpu.with_memory_space_constraint(x, pltpu.HBM) if spec is FAR else x
            for x, spec in zip(ins, specs)
        ]
    )


def gather(piece, axis, groups=None):
    count = len(groups[0]) if groups else lax.axis_size(axis)
    return lax.all_to_all(
        jnp.broadcast_to(piece[None], (count,) + piece.shape),
        axis, 0, 0, axis_index_groups=groups, tiled=True,
    )


def near_groups(tiles_x, tiles_y):
    every = np.arange(tiles_x * tiles_y).reshape(-1, 4, 2, tiles_y // 2, 2)
    along_gx = np.arange(tiles_x).reshape(-1, 4, 2)
    wide = along_gx.transpose(1, 0, 2).reshape(4, -1)
    tall = every.transpose(0, 2, 3, 1, 4).reshape(-1, 8)
    deep = np.arange(tiles_y).reshape(-1, 2).T
    return wide.tolist(), tall.tolist(), deep.tolist()


def swap(piece, axis, start):
    pairs = [(i, i + 1) for i in range(start, lax.axis_size(axis) - 1, 2)]
    return lax.ppermute(piece, axis, pairs + [(j, i) for i, j in pairs])


def per_device(fields, terrain, columns, record_tile, record_cells, record_weights):
    tiles_x, tiles_y = lax.axis_size("gx"), lax.axis_size("gy")
    variables, levels, cells_x, cells_y = fields.shape
    total_x, total_y = cells_x * tiles_x, cells_y * tiles_y
    coarse_x, coarse_y = cells_x // RATIO, cells_y // RATIO
    count = variables * levels
    wide = count * KW
    parents, records = columns.shape[1:]
    entries = record_cells.shape[1]
    scale = 1.0 / np.sqrt(total_x * total_y)
    per = LANES // KW
    f32, b16 = jnp.float32, jnp.bfloat16

    wave_x, wave_y = wave_rows(total_x), wave_rows(total_y)
    by_x = wave_x.reshape(KW, tiles_x, cells_x).transpose(1, 0, 2)
    by_y = wave_y.reshape(KW, tiles_y, cells_y).transpose(1, 0, 2)
    tab_bx = two_parts(by_x, -2)
    tab_byt = two_parts(np.tile(by_y.transpose(0, 2, 1), (1, 1, per)), -1)
    outer, inner = turns(cells_x * np.arange(tiles_x), RATIO * np.arange(coarse_x), total_x)
    tab_a = two_parts(outer, -2)
    tab_c = two_parts(np.pad(inner, ((0, 0), (0, -coarse_x % 16))), -2)
    tab_ay = np.tile(
        by_y[:, :, ::RATIO].transpose(0, 2, 1), (1, 1, LANES // coarse_y)
    ).astype(np.float32)
    tab_low_x = two_parts(-4.0 * scale * by_x.transpose(0, 2, 1), -1)
    tab_low_x = np.concatenate([tab_low_x, tab_low_x[..., :KW]], axis=-1)
    tab_low_y = two_parts(np.tile(by_y, (1, per, 1)), -2)
    tab_low_y = np.concatenate(
        [tab_low_y[:, :LANES], tab_low_y[:, :LANES], tab_low_y[:, LANES:]], axis=1
    )

    f = fields.reshape(count, cells_x, cells_y)
    coarse = coarse_x * coarse_y
    padded = -(-coarse // LANES) * LANES
    own = terrain[::RATIO, ::RATIO].astype(f32).reshape(coarse)
    own = jnp.pad(own, (0, padded - coarse)).reshape(padded // LANES, LANES)
    heights = gather(own, "gx").reshape(tiles_x, padded)

    tile, cells = record_tile.T, record_cells.T
    nest, look, xa, xb, ya, yb = call(
        functools.partial(ready_kernel, coarse_y=coarse_y),
        (f, tab_bx, tab_byt, tile, cells, tab_a, tab_c),
        [FAR] * 7,
        [((KW, wide), f32), ((2 * KW, entries * records), b16)] + [((count, cells_y), f32)] * 4,
        [NEAR] * 6,
        [
            pltpu.VMEM(f.shape, f32),
            pltpu.VMEM(tab_bx.shape[1:], b16),
            pltpu.VMEM(tab_byt.shape[1:], b16),
            pltpu.VMEM(tile.shape, jnp.int32),
            pltpu.VMEM(cells.shape, jnp.int32),
            pltpu.VMEM(tab_a.shape, b16),
            pltpu.VMEM(tab_c.shape, b16),
            DMA,
            DMA,
            DMA,
            DMA((4,)),
        ],
    )
    (part,) = call(
        functools.partial(record_kernel, levels=levels, coarse_y=coarse_y, scale=scale),
        (heights, tile, cells, record_weights.T, columns, look, nest, tab_ay),
        [NEAR] * 7 + [FAR],
        [((8, KW // 8 * wide // LANES, LANES), f32)],
        [NEAR],
        [
            pltpu.VMEM((variables, -(-parents // 8) * 8, records), f32),
            pltpu.VMEM((padded, records), f32),
            pltpu.VMEM((count * coarse_y, entries * records), b16),
            pltpu.VMEM((count * coarse_y, entries * records), b16),
            pltpu.VMEM(tab_ay.shape[1:], f32),
            DMA,
        ],
    )
    wide_groups, tall_groups, deep_groups = near_groups(tiles_x, tiles_y)
    pieces = part.reshape(len(wide_groups[0]), -1, LANES)
    mine = jnp.sum(
        lax.all_to_all(pieces, "gx", 0, 0, axis_index_groups=wide_groups, tiled=True).reshape(
            pieces.shape
        ),
        axis=0,
    )
    xa, xb, ya, yb, _ = lax.optimization_barrier((xa, xb, ya, yb, part))
    xa = swap(xa, "gx", 0)
    mine, xa, xb, ya, yb = lax.optimization_barrier((mine, xa, xb, ya, yb))
    xb = swap(xb, "gx", 1)
    mine = jnp.sum(gather(mine, ("gx", "gy"), tall_groups), axis=0)
    mine, xb, ya, yb = lax.optimization_barrier((mine, xb, ya, yb))
    yb, ya = swap(yb, "gy", 1), swap(ya, "gy", 0)
    mine = jnp.sum(gather(mine, "gy", deep_groups), axis=0)
    mine, ya, yb = lax.optimization_barrier((mine, ya, yb))
    nudge = gather(mine, "gx", wide_groups).reshape(part.shape)

    (state,) = call(
        functools.partial(stencil_kernel, variables=variables),
        (mine, f, terrain, xa, xb, ya, yb),
        [LOOSE] + [NEAR] * 6,
        [(f.shape, f32)],
        [NEAR],
        [pltpu.VMEM(xa.shape, f32)] * 2,
    )
    updated, coeffs = call(
        nudge_kernel,
        (state, nudge, tab_low_x, tab_low_y),
        [NEAR, NEAR, FAR, FAR],
        [(f.shape, f32), ((count, KW, KW), f32)],
        [FAR, FAR],
        [
            pltpu.VMEM(f.shape, f32),
            pltpu.VMEM((count, KW, KW), f32),
            pltpu.VMEM(tab_low_x.shape[1:], b16),
            pltpu.VMEM(tab_low_y.shape[1:], b16),
            pltpu.VMEM((count // per // 2 * cells_x, per * cells_y), f32),
            DMA((count // per,)),
            DMA,
            DMA,
            DMA,
        ],
    )
    return updated.reshape(fields.shape), coeffs.reshape(variables, levels, KW, KW)


def solution(mesh):
    return jax.shard_map(
        per_device,
        mesh=mesh,
        in_specs=(
            P(None, None, "gx", "gy"),
            P("gx", "gy"),
            P(None, None, ("gx", "gy")),
            P(("gx", "gy"), None),
            P(("gx", "gy"), None),
            P(("gx", "gy"), None),
        ),
        out_specs=(P(None, None, "gx", "gy"), P()),
        check_vma=False,
    )
```

```python
import functools

import jax
import jax.numpy as jnp
import numpy as np
from jax import lax
from jax.experimental import pallas as pl
from jax.experimental.pallas import tpu as pltpu
from jax.sharding import PartitionSpec as P

KW = 32
RATIO = 8
TOP = 12000.0
HIGHEST_CELL = 2999.0
LANES = 128
EXACT = lax.Precision.HIGHEST


def wave_rows(length):
    half = KW // 2
    x = np.arange(length)
    rows = [np.ones(length)]
    for m in range(1, half):
        rows.append(np.sqrt(2.0) * np.cos(2.0 * np.pi * (m * x % length) / length))
    for m in range(half, KW):
        rows.append(np.sqrt(2.0) * np.sin(2.0 * np.pi * ((m - half + 1) * x % length) / length))
    return np.stack(rows)


def turns(outer, inner, length):
    half = KW // 2
    wave = np.arange(KW)
    wave = np.where(wave < half, wave, wave - half + 1)[:, None]
    a = 2.0 * np.pi * (wave * outer[None, :] % length) / length
    c = 2.0 * np.pi * (wave * inner[None, :] % length) / length
    size = np.where(wave == 0, 1.0, np.sqrt(2.0))
    cosine = np.arange(KW)[:, None] < half
    with_cos = size * np.where(cosine, np.cos(a), np.sin(a))
    with_sin = size * np.where(cosine, -np.sin(a), np.cos(a))
    return np.concatenate([with_cos, with_sin]), np.concatenate([np.cos(c), np.sin(c)])


def two_parts(table, axis):
    whole = table.astype(np.float32)
    high = whole.astype(jnp.bfloat16)
    low = (whole - high.astype(np.float32)).astype(jnp.bfloat16)
    return np.concatenate([high, low], axis=axis)


def dot(a, b, dims=((1,), (0,)), precision=None):
    return lax.dot_general(
        a, b, (dims, ((), ())), precision=precision, preferred_element_type=jnp.float32
    )


def rows_lanes(shape):
    return (
        lax.broadcasted_iota(jnp.int32, shape, 0),
        lax.broadcasted_iota(jnp.int32, shape, 1),
    )


def split(x):
    high = x.astype(jnp.bfloat16)
    return high, (x - high.astype(jnp.float32)).astype(jnp.bfloat16)


def by_parity(axis, a, b):
    first = lax.rem(lax.axis_index(axis), 2) == 0
    return jnp.where(first, a, b), jnp.where(first, b, a)


def hot(mask):
    return jnp.where(mask, 1.0, 0.0).astype(jnp.bfloat16)


def ready_kernel(
    f_hbm, bx_hbm, by_hbm, tile_hbm, cells_hbm, taba_hbm, tabc_hbm, p_ref, look_ref,
    xa_ref, xb_ref, ya_ref, yb_ref, f_ref, bx_ref, by_ref, tile_ref, cells_ref, taba_ref, tabc_ref, f_sem, bx_sem, by_sem, small_sem,
    *, coarse_y
):
    count, cells_x, cells_y = f_ref.shape
    per = LANES // KW
    groups = count // per
    fetch = pltpu.make_async_copy(f_hbm, f_ref, f_sem)
    by_copy = pltpu.make_async_copy(by_hbm.at[lax.axis_index("gy")], by_ref, by_sem)
    bx_copy = pltpu.make_async_copy(bx_hbm.at[lax.axis_index("gx")], bx_ref, bx_sem)
    small = [
        pltpu.make_async_copy(a, b, small_sem.at[i])
        for i, (a, b) in enumerate(
            (
                (tile_hbm, tile_ref),
                (cells_hbm, cells_ref),
                (taba_hbm, taba_ref),
                (tabc_hbm, tabc_ref),
            )
        )
    ]
    for copy in (*small, by_copy, fetch, bx_copy):
        copy.start()
    for copy in small:
        copy.wait()
    records = tile_ref.shape[1]
    row_t, _ = rows_lanes((taba_ref.shape[1], records))
    row_c, _ = rows_lanes((tabc_ref.shape[1], records))
    both = dot(taba_ref[...], hot(row_t == tile_ref[...]))
    outer = both[: 2 * KW] + both[2 * KW :]
    cells = cells_ref[...] // coarse_y
    for e in range(cells_ref.shape[0]):
        both = dot(tabc_ref[...], hot(row_c == cells[e : e + 1, :]))
        inner = both[: 2 * KW] + both[2 * KW :]
        turned = outer * inner
        high, low = split(turned[:KW] + turned[KW:])
        look_ref[:KW, e * records : (e + 1) * records] = high
        look_ref[KW:, e * records : (e + 1) * records] = low
    by_copy.wait()
    by4 = by_ref[...].astype(jnp.float32)
    _, lane = rows_lanes(by4.shape)
    spread = jnp.concatenate(
        [
            jnp.where(lane % LANES // KW == q, by4, 0.0).astype(jnp.bfloat16)
            for q in range(per)
        ],
        axis=0,
    )
    fetch.wait()
    bx_copy.wait()
    values = jnp.concatenate(
        [
            jnp.concatenate([f_ref[per * g + q] for q in range(per)], axis=1)
            for g in range(groups)
        ],
        axis=0,
    )
    high, low = split(values)
    both = dot(high, spread)
    along = both[:, :LANES] + both[:, LANES:] + dot(low, spread[:, :LANES])
    high, low = split(
        jnp.concatenate([along[g * cells_x : (g + 1) * cells_x] for g in range(groups)], axis=1)
    )
    both = dot(bx_ref[...], high)
    p_ref[...] = both[:KW] + both[KW:] + dot(bx_ref[:KW, :], low)
    row, lane = rows_lanes((cells_x, cells_y))
    for i in range(count):
        for ref, at in ((xa_ref, cells_x - 1), (xb_ref, 0)):
            ref[i : i + 1, :] = f_ref[i, at : at + 1, :]
        for ref, at in ((ya_ref, cells_y - 1), (yb_ref, 0)):
            edge = jnp.broadcast_to(f_ref[i, :, at : at + 1], (cells_x, cells_y))
            ref[i : i + 1, :] = jnp.sum(jnp.where(row == lane, edge, 0.0), axis=0, keepdims=True)
    for axis, a_ref, b_ref in (("gx", xa_ref, xb_ref), ("gy", ya_ref, yb_ref)):
        a_ref[...], b_ref[...] = by_parity(axis, a_ref[...], b_ref[...])


def reach(k, levels, parents, highest):
    bottoms = [h + (k - 0.5) * (TOP - h) / levels for h in (0.0, highest)]
    tops = [h + (k + 1.5) * (TOP - h) / levels for h in (0.0, highest)]
    step = TOP / parents
    first = int(np.floor((min(bottoms) - 1.0) / step - 0.5))
    last = int(np.ceil((max(tops) + 1.0) / step - 0.5)) + 1
    return max(0, first) // 8 * 8, min(-(-parents // 8), -(-last // 8)) * 8


def record_kernel(
    h_ref, tile_ref, cells_ref, weights_ref, cols_ref, look_ref, p_ref, taby_hbm, d_ref,
    col_ref, pick_ref, high_ref, low_ref, taby_ref, sem, *, levels, coarse_y, scale
):
    variables, parents, records = cols_ref.shape
    tiles, padded = h_ref.shape
    count = variables * levels
    fetch = pltpu.make_async_copy(taby_hbm.at[lax.axis_index("gy")], taby_ref, sem)
    fetch.start()
    tile = tile_ref[...]
    row, _ = rows_lanes((tiles, records))
    tile_hot = hot(row == tile)
    heights = h_ref[...]
    high = jnp.floor(heights * (1.0 / 64.0))
    low = heights - 64.0 * high
    over = ((0,), (0,))
    pick_ref[...] = 64.0 * dot(high.astype(jnp.bfloat16), tile_hot, over) + dot(
        low.astype(jnp.bfloat16), tile_hot, over
    )
    col_ref[...] = jnp.zeros_like(col_ref)
    for v in range(variables):
        col_ref[v, :parents, :] = cols_ref[v].astype(jnp.float32)
    row_c, _ = rows_lanes((padded, records))
    row_b, _ = rows_lanes((coarse_y, records))
    row_p, _ = rows_lanes(col_ref.shape[1:])
    parent = jnp.where(row_p < parents, (row_p.astype(jnp.float32) + 0.5) * (TOP / parents), 1e9)
    cells = cells_ref[...]
    weights = weights_ref[...].astype(jnp.float32)
    for e in range(cells_ref.shape[0]):
        at = slice(e * records, (e + 1) * records)
        cell = cells[e : e + 1, :]
        height = jnp.sum(jnp.where(row_c == cell, pick_ref[...], 0.0), axis=0, keepdims=True)
        in_b = row_b == cell % coarse_y
        inverse = levels / (TOP - height)
        shift_k = height * inverse + 0.5
        apart = parent * inverse - shift_k
        for k in range(levels):
            first, last = reach(k, levels, parents, HIGHEST_CELL)
            hat = jnp.maximum(0.0, 1.0 - jnp.abs(apart[first:last] - float(k)))
            share = weights[e : e + 1, :] / jnp.sum(hat, axis=0, keepdims=True)
            for v in range(variables):
                value = jnp.sum(hat * col_ref[v, first:last, :], axis=0, keepdims=True) * share
                rest = value - value.astype(jnp.bfloat16).astype(jnp.float32)
                i = (v * levels + k) * coarse_y
                high_ref[i : i + coarse_y, at] = jnp.where(in_b, value, 0.0).astype(jnp.bfloat16)
                low_ref[i : i + coarse_y, at] = jnp.where(in_b, rest, 0.0).astype(jnp.bfloat16)
    last = ((1,), (1,))
    both = dot(high_ref[...], look_ref[...], last)
    by_b = both[:, :KW] + both[:, KW:] + dot(low_ref[...], look_ref[:KW, :], last)
    some = LANES // coarse_y
    groups = count // some
    fetch.wait()
    taby = taby_ref[...].astype(jnp.float32)
    tall = jnp.concatenate([taby] * some, axis=0)
    row, lane = rows_lanes(tall.shape)
    width = some * KW
    tall = jnp.where(row // coarse_y == lane % width // KW, tall, 0.0).astype(jnp.bfloat16)
    turned = jnp.concatenate(
        [jnp.transpose(by_b[g * LANES : (g + 1) * LANES]) for g in range(groups)], axis=0
    )
    high, low = split(turned)
    both = dot(high, tall)
    targets = both[:, :width] + both[:, width:] + dot(low, tall[:, :width])
    for g in range(groups):
        target = targets[g * KW : (g + 1) * KW]
        for i in range(some * KW // LANES):
            j = g * (some * KW // LANES) + i
            here = slice(j * LANES, (j + 1) * LANES)
            part = p_ref[:, here] * scale - target[:, i * LANES : (i + 1) * LANES] * (
                RATIO * RATIO * scale
            )
            for m in range(KW // 8):
                d_ref[:, m * p_ref.shape[1] // LANES + j, :] = part[8 * m : 8 * m + 8]


def stencil_kernel(
    after, f_ref, terrain_ref, xa_ref, xb_ref, ya_ref, yb_ref, bx_hbm, by_hbm, out_ref, bx_ref, right_ref,
    east_ref, west_ref, by_ref, bx_sem, by_sem, *, variables
):
    bx_copy = pltpu.make_async_copy(bx_hbm.at[lax.axis_index("gx")], bx_ref, bx_sem)
    by_copy = pltpu.make_async_copy(by_hbm.at[lax.axis_index("gy")], by_ref, by_sem)
    bx_copy.start()
    by_copy.start()
    count, cells_x, cells_y = f_ref.shape
    levels = count // variables
    row, lane = rows_lanes((cells_x, cells_y))
    east_ref[...], west_ref[...] = by_parity("gx", xa_ref[...], xb_ref[...])
    north, south = by_parity("gy", ya_ref[...], yb_ref[...])
    south = jnp.transpose(south)
    north = jnp.transpose(north)
    metric = TOP / (TOP - terrain_ref[...].astype(jnp.float32))
    metric = metric * metric * 0.1
    for i in range(count):
        k = i % levels
        q = f_ref[i]
        wind_x = f_ref[k]
        wind_y = f_ref[levels + k]
        east = jnp.where(row == cells_x - 1, east_ref[i : i + 1, :], pltpu.roll(q, cells_x - 1, 0))
        west = jnp.where(row == 0, west_ref[i : i + 1, :], pltpu.roll(q, 1, 0))
        above = jnp.where(
            lane == cells_y - 1, north[:cells_x, i : i + 1], pltpu.roll(q, cells_y - 1, 1)
        )
        below = jnp.where(lane == 0, south[:cells_x, i : i + 1], pltpu.roll(q, 1, 1))
        transport = wind_x * (east - west) + wind_y * (above - below)
        diffusion = east + west + above + below - 4.0 * q
        upper = f_ref[i + 1] if k < levels - 1 else q
        lower = f_ref[i - 1] if k > 0 else q
        mixing = (upper - 2.0 * q + lower) * metric
        out_ref[i] = q - 0.05 * transport + 0.1 * diffusion + mixing
    by_copy.wait()
    by4 = by_ref[...].astype(jnp.float32)
    block, _ = rows_lanes(by4.shape)
    for q in range(LANES // KW):
        right_ref[:, q * cells_y : (q + 1) * cells_y] = jnp.where(
            block % LANES // KW == q, by4, 0.0
        ).astype(jnp.bfloat16)
    bx_copy.wait()


def nudge_kernel(
    state_ref, n_ref, bx_ref, right_ref, out_hbm, coeffs_hbm, out_ref, coeffs_ref, low_ref, out_sem, coeffs_sem
):
    count, cells_x, cells_y = state_ref.shape
    per = LANES // KW
    groups = count // per
    nudge = jnp.concatenate(
        [
            jnp.concatenate([n_ref[:, m * groups + g, :] for m in range(KW // 8)], axis=0)
            for g in range(groups)
        ],
        axis=1,
    )
    high, low = split(nudge)
    along = dot(bx_ref[...], jnp.concatenate([high, high, low], axis=0))
    high, low = split(along)
    for i in range(count):
        coeffs_ref[i] = nudge[:, i * KW : (i + 1) * KW]
    copies = [pltpu.make_async_copy(coeffs_ref, coeffs_hbm, coeffs_sem)]
    copies[0].start()
    thirds = 3
    some = groups // thirds
    for third in range(thirds):
        left = jnp.concatenate(
            [
                jnp.concatenate([x[:, g * LANES : (g + 1) * LANES] for x in (high, low, high)], axis=1)
                for g in range(third * some, (third + 1) * some)
            ],
            axis=0,
        )
        low_ref[...] = dot(left, right_ref[...])
        for g in range(some):
            for q in range(per):
                i = per * (third * some + g) + q
                out_ref[i] = state_ref[i] + low_ref[
                    g * cells_x : (g + 1) * cells_x, q * cells_y : (q + 1) * cells_y
                ]
            at = pl.ds(per * (third * some + g), per)
            copies.append(
                pltpu.make_async_copy(out_ref.at[at], out_hbm.at[at], out_sem.at[third * some + g])
            )
            copies[-1].start()
    for copy in copies:
        copy.wait()


FAR = pl.BlockSpec(memory_space=pltpu.HBM)
LOOSE = pl.BlockSpec(memory_space=pl.ANY)
NEAR = pl.BlockSpec(memory_space=pltpu.VMEM)
DMA = pltpu.SemaphoreType.DMA


def call(kernel, ins, specs, outs, out_specs, scratch=()):
    return pl.pallas_call(
        kernel,
        out_shape=[jax.ShapeDtypeStruct(s, d) for s, d in outs],
        in_specs=specs,
        out_specs=out_specs,
        scratch_shapes=list(scratch),
        compiler_params=pltpu.CompilerParams(vmem_limit_bytes=48 << 20),
    )(
        *[
            pltpu.with_memory_space_constraint(x, pltpu.HBM) if spec is FAR else x
            for x, spec in zip(ins, specs)
        ]
    )


def gather(piece, axis, groups=None):
    count = len(groups[0]) if groups else lax.axis_size(axis)
    return lax.all_to_all(
        jnp.broadcast_to(piece[None], (count,) + piece.shape),
        axis, 0, 0, axis_index_groups=groups, tiled=True,
    )


def near_groups(tiles_x, tiles_y):
    every = np.arange(tiles_x * tiles_y).reshape(-1, 4, 2, tiles_y // 2, 2)
    along_gx = np.arange(tiles_x).reshape(-1, 4, 2)
    wide = along_gx.transpose(1, 0, 2).reshape(4, -1)
    tall = every.transpose(0, 2, 3, 1, 4).reshape(-1, 8)
    deep = np.arange(tiles_y).reshape(-1, 2).T
    return wide.tolist(), tall.tolist(), deep.tolist()


def swap(piece, axis, start):
    pairs = [(i, i + 1) for i in range(start, lax.axis_size(axis) - 1, 2)]
    return lax.ppermute(piece, axis, pairs + [(j, i) for i, j in pairs])


def per_device(fields, terrain, columns, record_tile, record_cells, record_weights):
    tiles_x, tiles_y = lax.axis_size("gx"), lax.axis_size("gy")
    variables, levels, cells_x, cells_y = fields.shape
    total_x, total_y = cells_x * tiles_x, cells_y * tiles_y
    coarse_x, coarse_y = cells_x // RATIO, cells_y // RATIO
    count = variables * levels
    wide = count * KW
    parents, records = columns.shape[1:]
    entries = record_cells.shape[1]
    scale = 1.0 / np.sqrt(total_x * total_y)
    per = LANES // KW
    f32, b16 = jnp.float32, jnp.bfloat16

    wave_x, wave_y = wave_rows(total_x), wave_rows(total_y)
    by_x = wave_x.reshape(KW, tiles_x, cells_x).transpose(1, 0, 2)
    by_y = wave_y.reshape(KW, tiles_y, cells_y).transpose(1, 0, 2)
    tab_bx = two_parts(by_x, -2)
    tab_byt = two_parts(np.tile(by_y.transpose(0, 2, 1), (1, 1, per)), -1)
    outer, inner = turns(cells_x * np.arange(tiles_x), RATIO * np.arange(coarse_x), total_x)
    tab_a = two_parts(outer, -2)
    tab_c = two_parts(np.pad(inner, ((0, 0), (0, -coarse_x % 16))), -2)
    tab_ay = two_parts(
        np.tile(by_y[:, :, ::RATIO].transpose(0, 2, 1), (1, 1, LANES // coarse_y)), -1
    )
    tab_low_x = two_parts(-4.0 * scale * by_x.transpose(0, 2, 1), -1)
    tab_low_x = np.concatenate([tab_low_x, tab_low_x[..., :KW]], axis=-1)
    tab_low_y = two_parts(np.tile(by_y, (1, per, 1)), -2)
    tab_low_y = np.concatenate(
        [tab_low_y[:, :LANES], tab_low_y[:, :LANES], tab_low_y[:, LANES:]], axis=1
    )

    f = fields.reshape(count, cells_x, cells_y)
    coarse = coarse_x * coarse_y
    padded = -(-coarse // LANES) * LANES
    own = terrain[::RATIO, ::RATIO].astype(f32).reshape(coarse)
    own = jnp.pad(own, (0, padded - coarse)).reshape(padded // LANES, LANES)
    heights = gather(own, "gx").reshape(tiles_x, padded)

    tile, cells = record_tile.T, record_cells.T
    nest, look, xa, xb, ya, yb = call(
        functools.partial(ready_kernel, coarse_y=coarse_y),
        (f, tab_bx, tab_byt, tile, cells, tab_a, tab_c),
        [FAR] * 7,
        [((KW, wide), f32), ((2 * KW, entries * records), b16)] + [((count, cells_y), f32)] * 4,
        [NEAR] * 6,
        [
            pltpu.VMEM(f.shape, f32),
            pltpu.VMEM(tab_bx.shape[1:], b16),
            pltpu.VMEM(tab_byt.shape[1:], b16),
            pltpu.VMEM(tile.shape, jnp.int32),
            pltpu.VMEM(cells.shape, jnp.int32),
            pltpu.VMEM(tab_a.shape, b16),
            pltpu.VMEM(tab_c.shape, b16),
            DMA,
            DMA,
            DMA,
            DMA((4,)),
        ],
    )
    (part,) = call(
        functools.partial(record_kernel, levels=levels, coarse_y=coarse_y, scale=scale),
        (heights, tile, cells, record_weights.T, columns, look, nest, tab_ay),
        [NEAR] * 7 + [FAR],
        [((8, KW // 8 * wide // LANES, LANES), f32)],
        [NEAR],
        [
            pltpu.VMEM((variables, -(-parents // 8) * 8, records), f32),
            pltpu.VMEM((padded, records), f32),
            pltpu.VMEM((count * coarse_y, entries * records), b16),
            pltpu.VMEM((count * coarse_y, entries * records), b16),
            pltpu.VMEM(tab_ay.shape[1:], b16),
            DMA,
        ],
    )
    wide_groups, tall_groups, deep_groups = near_groups(tiles_x, tiles_y)
    pieces = part.reshape(len(wide_groups[0]), -1, LANES)
    mine = jnp.sum(
        lax.all_to_all(pieces, "gx", 0, 0, axis_index_groups=wide_groups, tiled=True).reshape(
            pieces.shape
        ),
        axis=0,
    )
    mine, xa, xb, ya, yb = lax.optimization_barrier((mine, xa, xb, ya, yb))
    ya, xa = swap(ya, "gy", 0), swap(xa, "gx", 0)
    mine = jnp.sum(gather(mine, ("gx", "gy"), tall_groups), axis=0)
    mine, xa, xb, ya, yb = lax.optimization_barrier((mine, xa, xb, ya, yb))
    xb, yb = swap(xb, "gx", 1), swap(yb, "gy", 1)
    mine = jnp.sum(gather(mine, "gy", deep_groups), axis=0)
    mine, xb, yb = lax.optimization_barrier((mine, xb, yb))
    nudge = gather(mine, "gx", wide_groups).reshape(part.shape)

    state, low_x, low_y = call(
        functools.partial(stencil_kernel, variables=variables),
        (mine, f, terrain, xa, xb, ya, yb, tab_low_x, tab_low_y),
        [LOOSE] + [NEAR] * 6 + [FAR] * 2,
        [
            (f.shape, f32),
            (tab_low_x.shape[1:], b16),
            (tab_low_y.shape[1:2] + (per * cells_y,), b16),
        ],
        [NEAR] * 3,
        [pltpu.VMEM(xa.shape, f32)] * 2 + [pltpu.VMEM(tab_low_y.shape[1:], b16), DMA, DMA],
    )
    updated, coeffs = call(
        nudge_kernel,
        (state, nudge, low_x, low_y),
        [NEAR] * 4,
        [(f.shape, f32), ((count, KW, KW), f32)],
        [FAR, FAR],
        [
            pltpu.VMEM(f.shape, f32),
            pltpu.VMEM((count, KW, KW), f32),
            pltpu.VMEM((count // per // 3 * cells_x, per * cells_y), f32),
            DMA((count // per,)),
            DMA,
        ],
    )
    return updated.reshape(fields.shape), coeffs.reshape(variables, levels, KW, KW)


def solution(mesh):
    return jax.shard_map(
        per_device,
        mesh=mesh,
        in_specs=(
            P(None, None, "gx", "gy"),
            P("gx", "gy"),
            P(None, None, ("gx", "gy")),
            P(("gx", "gy"), None),
            P(("gx", "gy"), None),
            P(("gx", "gy"), None),
        ),
        out_specs=(P(None, None, "gx", "gy"), P()),
        check_vma=False,
    )
```

```python
import functools

import jax
import jax.numpy as jnp
import numpy as np
from jax import lax
from jax.experimental import pallas as pl
from jax.experimental.pallas import tpu as pltpu
from jax.sharding import PartitionSpec as P

KW = 32
RATIO = 8
TOP = 12000.0
HIGHEST_CELL = 2999.0
LANES = 128
EXACT = lax.Precision.HIGHEST


def wave_rows(length):
    half = KW // 2
    x = np.arange(length)
    rows = [np.ones(length)]
    for m in range(1, half):
        rows.append(np.sqrt(2.0) * np.cos(2.0 * np.pi * (m * x % length) / length))
    for m in range(half, KW):
        rows.append(np.sqrt(2.0) * np.sin(2.0 * np.pi * ((m - half + 1) * x % length) / length))
    return np.stack(rows)


def turns(outer, inner, length):
    half = KW // 2
    wave = np.arange(KW)
    wave = np.where(wave < half, wave, wave - half + 1)[:, None]
    a = 2.0 * np.pi * (wave * outer[None, :] % length) / length
    c = 2.0 * np.pi * (wave * inner[None, :] % length) / length
    size = np.where(wave == 0, 1.0, np.sqrt(2.0))
    cosine = np.arange(KW)[:, None] < half
    with_cos = size * np.where(cosine, np.cos(a), np.sin(a))
    with_sin = size * np.where(cosine, -np.sin(a), np.cos(a))
    return np.concatenate([with_cos, with_sin]), np.concatenate([np.cos(c), np.sin(c)])


def two_parts(table, axis):
    whole = table.astype(np.float32)
    high = whole.astype(jnp.bfloat16)
    low = (whole - high.astype(np.float32)).astype(jnp.bfloat16)
    return np.concatenate([high, low], axis=axis)


def dot(a, b, dims=((1,), (0,)), precision=None):
    return lax.dot_general(
        a, b, (dims, ((), ())), precision=precision, preferred_element_type=jnp.float32
    )


def rows_lanes(shape):
    return (
        lax.broadcasted_iota(jnp.int32, shape, 0),
        lax.broadcasted_iota(jnp.int32, shape, 1),
    )


def split(x):
    high = x.astype(jnp.bfloat16)
    return high, (x - high.astype(jnp.float32)).astype(jnp.bfloat16)


def by_parity(axis, a, b):
    first = lax.rem(lax.axis_index(axis), 2) == 0
    return jnp.where(first, a, b), jnp.where(first, b, a)


def hot(mask):
    return jnp.where(mask, 1.0, 0.0).astype(jnp.bfloat16)


def ready_kernel(
    f_hbm, bx_hbm, by_hbm, tile_hbm, cells_hbm, taba_hbm, tabc_hbm, p_ref, look_ref,
    xa_ref, xb_ref, ya_ref, yb_ref, f_ref, bx_ref, by_ref, tile_ref, cells_ref, taba_ref, tabc_ref, f_sem, bx_sem, by_sem, small_sem,
    *, coarse_y
):
    count, cells_x, cells_y = f_ref.shape
    per = LANES // KW
    groups = count // per
    fetch = pltpu.make_async_copy(f_hbm, f_ref, f_sem)
    by_copy = pltpu.make_async_copy(by_hbm.at[lax.axis_index("gy")], by_ref, by_sem)
    bx_copy = pltpu.make_async_copy(bx_hbm.at[lax.axis_index("gx")], bx_ref, bx_sem)
    small = [
        pltpu.make_async_copy(a, b, small_sem.at[i])
        for i, (a, b) in enumerate(
            (
                (tile_hbm, tile_ref),
                (cells_hbm, cells_ref),
                (taba_hbm, taba_ref),
                (tabc_hbm, tabc_ref),
            )
        )
    ]
    for copy in (*small, by_copy, fetch, bx_copy):
        copy.start()
    for copy in small:
        copy.wait()
    records = tile_ref.shape[1]
    row_t, _ = rows_lanes((taba_ref.shape[1], records))
    row_c, _ = rows_lanes((tabc_ref.shape[1], records))
    both = dot(taba_ref[...], hot(row_t == tile_ref[...]))
    outer = both[: 2 * KW] + both[2 * KW :]
    cells = cells_ref[...] // coarse_y
    for e in range(cells_ref.shape[0]):
        both = dot(tabc_ref[...], hot(row_c == cells[e : e + 1, :]))
        inner = both[: 2 * KW] + both[2 * KW :]
        turned = outer * inner
        high, low = split(turned[:KW] + turned[KW:])
        look_ref[:KW, e * records : (e + 1) * records] = high
        look_ref[KW:, e * records : (e + 1) * records] = low
    by_copy.wait()
    by4 = by_ref[...].astype(jnp.float32)
    _, lane = rows_lanes(by4.shape)
    spread = jnp.concatenate(
        [
            jnp.where(lane % LANES // KW == q, by4, 0.0).astype(jnp.bfloat16)
            for q in range(per)
        ],
        axis=0,
    )
    fetch.wait()
    bx_copy.wait()
    values = jnp.concatenate(
        [
            jnp.concatenate([f_ref[per * g + q] for q in range(per)], axis=1)
            for g in range(groups)
        ],
        axis=0,
    )
    high, low = split(values)
    both = dot(high, spread)
    along = both[:, :LANES] + both[:, LANES:] + dot(low, spread[:, :LANES])
    high, low = split(
        jnp.concatenate([along[g * cells_x : (g + 1) * cells_x] for g in range(groups)], axis=1)
    )
    both = dot(bx_ref[...], high)
    p_ref[...] = both[:KW] + both[KW:] + dot(bx_ref[:KW, :], low)
    row, lane = rows_lanes((cells_x, cells_y))
    for i in range(count):
        for ref, at in ((xa_ref, cells_x - 1), (xb_ref, 0)):
            ref[i : i + 1, :] = f_ref[i, at : at + 1, :]
        for ref, at in ((ya_ref, cells_y - 1), (yb_ref, 0)):
            edge = jnp.broadcast_to(f_ref[i, :, at : at + 1], (cells_x, cells_y))
            ref[i : i + 1, :] = jnp.sum(jnp.where(row == lane, edge, 0.0), axis=0, keepdims=True)
    for axis, a_ref, b_ref in (("gx", xa_ref, xb_ref), ("gy", ya_ref, yb_ref)):
        a_ref[...], b_ref[...] = by_parity(axis, a_ref[...], b_ref[...])


def reach(k, levels, parents, highest):
    bottoms = [h + (k - 0.5) * (TOP - h) / levels for h in (0.0, highest)]
    tops = [h + (k + 1.5) * (TOP - h) / levels for h in (0.0, highest)]
    step = TOP / parents
    first = int(np.floor((min(bottoms) - 1.0) / step - 0.5))
    last = int(np.ceil((max(tops) + 1.0) / step - 0.5)) + 1
    return max(0, first) // 8 * 8, min(-(-parents // 8), -(-last // 8)) * 8


def record_kernel(
    h_ref, tile_ref, cells_ref, weights_ref, cols_ref, look_ref, p_ref, taby_hbm, d_ref,
    col_ref, pick_ref, high_ref, low_ref, taby_ref, sem, *, levels, coarse_y, scale
):
    variables, parents, records = cols_ref.shape
    tiles, padded = h_ref.shape
    count = variables * levels
    fetch = pltpu.make_async_copy(taby_hbm.at[lax.axis_index("gy")], taby_ref, sem)
    fetch.start()
    tile = tile_ref[...]
    row, _ = rows_lanes((tiles, records))
    tile_hot = hot(row == tile)
    heights = h_ref[...]
    high = jnp.floor(heights * (1.0 / 64.0))
    low = heights - 64.0 * high
    over = ((0,), (0,))
    pick_ref[...] = 64.0 * dot(high.astype(jnp.bfloat16), tile_hot, over) + dot(
        low.astype(jnp.bfloat16), tile_hot, over
    )
    col_ref[...] = jnp.zeros_like(col_ref)
    for v in range(variables):
        col_ref[v, :parents, :] = cols_ref[v].astype(jnp.float32)
    row_c, _ = rows_lanes((padded, records))
    row_b, _ = rows_lanes((coarse_y, records))
    row_p, _ = rows_lanes(col_ref.shape[1:])
    parent = jnp.where(row_p < parents, (row_p.astype(jnp.float32) + 0.5) * (TOP / parents), 1e9)
    cells = cells_ref[...]
    weights = weights_ref[...].astype(jnp.float32)
    for e in range(cells_ref.shape[0]):
        at = slice(e * records, (e + 1) * records)
        cell = cells[e : e + 1, :]
        height = jnp.sum(jnp.where(row_c == cell, pick_ref[...], 0.0), axis=0, keepdims=True)
        in_b = row_b == cell % coarse_y
        inverse = levels / (TOP - height)
        shift_k = height * inverse + 0.5
        apart = parent * inverse - shift_k
        for k in range(levels):
            first, last = reach(k, levels, parents, HIGHEST_CELL)
            hat = jnp.maximum(0.0, 1.0 - jnp.abs(apart[first:last] - float(k)))
            share = weights[e : e + 1, :] / jnp.sum(hat, axis=0, keepdims=True)
            for v in range(variables):
                value = jnp.sum(hat * col_ref[v, first:last, :], axis=0, keepdims=True) * share
                rest = value - value.astype(jnp.bfloat16).astype(jnp.float32)
                i = (v * levels + k) * coarse_y
                high_ref[i : i + coarse_y, at] = jnp.where(in_b, value, 0.0).astype(jnp.bfloat16)
                low_ref[i : i + coarse_y, at] = jnp.where(in_b, rest, 0.0).astype(jnp.bfloat16)
    last = ((1,), (1,))
    both = dot(high_ref[...], look_ref[...], last)
    by_b = both[:, :KW] + both[:, KW:] + dot(low_ref[...], look_ref[:KW, :], last)
    some = LANES // coarse_y
    groups = count // some
    fetch.wait()
    taby = taby_ref[...].astype(jnp.float32)
    tall = jnp.concatenate([taby] * some, axis=0)
    row, lane = rows_lanes(tall.shape)
    width = some * KW
    tall = jnp.where(row // coarse_y == lane % width // KW, tall, 0.0).astype(jnp.bfloat16)
    turned = jnp.concatenate(
        [jnp.transpose(by_b[g * LANES : (g + 1) * LANES]) for g in range(groups)], axis=0
    )
    high, low = split(turned)
    both = dot(high, tall)
    targets = both[:, :width] + both[:, width:] + dot(low, tall[:, :width])
    for g in range(groups):
        target = targets[g * KW : (g + 1) * KW]
        for i in range(some * KW // LANES):
            j = g * (some * KW // LANES) + i
            here = slice(j * LANES, (j + 1) * LANES)
            part = p_ref[:, here] * scale - target[:, i * LANES : (i + 1) * LANES] * (
                RATIO * RATIO * scale
            )
            for m in range(KW // 8):
                d_ref[:, m * p_ref.shape[1] // LANES + j, :] = part[8 * m : 8 * m + 8]


def stencil_kernel(
    after, f_ref, terrain_ref, xa_ref, xb_ref, ya_ref, yb_ref, bx_hbm, by_hbm, out_ref, bx_ref, right_ref,
    east_ref, west_ref, by_ref, bx_sem, by_sem, *, variables
):
    bx_copy = pltpu.make_async_copy(bx_hbm.at[lax.axis_index("gx")], bx_ref, bx_sem)
    by_copy = pltpu.make_async_copy(by_hbm.at[lax.axis_index("gy")], by_ref, by_sem)
    bx_copy.start()
    by_copy.start()
    count, cells_x, cells_y = f_ref.shape
    levels = count // variables
    row, lane = rows_lanes((cells_x, cells_y))
    east_ref[...], west_ref[...] = by_parity("gx", xa_ref[...], xb_ref[...])
    north, south = by_parity("gy", ya_ref[...], yb_ref[...])
    south = jnp.transpose(south)
    north = jnp.transpose(north)
    metric = TOP / (TOP - terrain_ref[...].astype(jnp.float32))
    metric = metric * metric * 0.1
    for i in range(count):
        k = i % levels
        q = f_ref[i]
        wind_x = f_ref[k]
        wind_y = f_ref[levels + k]
        east = jnp.where(row == cells_x - 1, east_ref[i : i + 1, :], pltpu.roll(q, cells_x - 1, 0))
        west = jnp.where(row == 0, west_ref[i : i + 1, :], pltpu.roll(q, 1, 0))
        above = jnp.where(
            lane == cells_y - 1, north[:cells_x, i : i + 1], pltpu.roll(q, cells_y - 1, 1)
        )
        below = jnp.where(lane == 0, south[:cells_x, i : i + 1], pltpu.roll(q, 1, 1))
        transport = wind_x * (east - west) + wind_y * (above - below)
        diffusion = east + west + above + below - 4.0 * q
        upper = f_ref[i + 1] if k < levels - 1 else q
        lower = f_ref[i - 1] if k > 0 else q
        mixing = (upper - 2.0 * q + lower) * metric
        out_ref[i] = q - 0.05 * transport + 0.1 * diffusion + mixing
    by_copy.wait()
    by4 = by_ref[...].astype(jnp.float32)
    block, _ = rows_lanes(by4.shape)
    for q in range(LANES // KW):
        right_ref[:, q * cells_y : (q + 1) * cells_y] = jnp.where(
            block % LANES // KW == q, by4, 0.0
        ).astype(jnp.bfloat16)
    bx_copy.wait()


def nudge_kernel(
    state_ref, n_ref, bx_ref, right_ref, out_hbm, coeffs_hbm, out_ref, coeffs_ref, low_ref, out_sem, coeffs_sem
):
    count, cells_x, cells_y = state_ref.shape
    per = LANES // KW
    groups = count // per
    nudge = jnp.concatenate(
        [
            jnp.concatenate([n_ref[:, m * groups + g, :] for m in range(KW // 8)], axis=0)
            for g in range(groups)
        ],
        axis=1,
    )
    high, low = split(nudge)
    along = dot(bx_ref[...], jnp.concatenate([high, high, low], axis=0))
    high, low = split(along)
    for i in range(count):
        coeffs_ref[i] = nudge[:, i * KW : (i + 1) * KW]
    copies = [pltpu.make_async_copy(coeffs_ref, coeffs_hbm, coeffs_sem)]
    copies[0].start()
    thirds = 3
    some = groups // thirds
    for third in range(thirds):
        left = jnp.concatenate(
            [
                jnp.concatenate([x[:, g * LANES : (g + 1) * LANES] for x in (high, low, high)], axis=1)
                for g in range(third * some, (third + 1) * some)
            ],
            axis=0,
        )
        low_ref[...] = dot(left, right_ref[...])
        for g in range(some):
            for q in range(per):
                i = per * (third * some + g) + q
                out_ref[i] = state_ref[i] + low_ref[
                    g * cells_x : (g + 1) * cells_x, q * cells_y : (q + 1) * cells_y
                ]
            at = pl.ds(per * (third * some + g), per)
            copies.append(
                pltpu.make_async_copy(out_ref.at[at], out_hbm.at[at], out_sem.at[third * some + g])
            )
            copies[-1].start()
    for copy in copies:
        copy.wait()


FAR = pl.BlockSpec(memory_space=pltpu.HBM)
LOOSE = pl.BlockSpec(memory_space=pl.ANY)
NEAR = pl.BlockSpec(memory_space=pltpu.VMEM)
DMA = pltpu.SemaphoreType.DMA


def call(kernel, ins, specs, outs, out_specs, scratch=()):
    return pl.pallas_call(
        kernel,
        out_shape=[jax.ShapeDtypeStruct(s, d) for s, d in outs],
        in_specs=specs,
        out_specs=out_specs,
        scratch_shapes=list(scratch),
        compiler_params=pltpu.CompilerParams(vmem_limit_bytes=48 << 20),
    )(
        *[
            pltpu.with_memory_space_constraint(x, pltpu.HBM) if spec is FAR else x
            for x, spec in zip(ins, specs)
        ]
    )


def gather(piece, axis, groups=None):
    count = len(groups[0]) if groups else lax.axis_size(axis)
    return lax.all_to_all(
        jnp.broadcast_to(piece[None], (count,) + piece.shape),
        axis, 0, 0, axis_index_groups=groups, tiled=True,
    )


def near_groups(tiles_x, tiles_y):
    every = np.arange(tiles_x * tiles_y).reshape(-1, 4, 2, tiles_y // 2, 2)
    along_gx = np.arange(tiles_x).reshape(-1, 4, 2)
    wide = along_gx.transpose(1, 0, 2).reshape(4, -1)
    tall = every.transpose(0, 2, 3, 1, 4).reshape(-1, 8)
    deep = np.arange(tiles_y).reshape(-1, 2).T
    return wide.tolist(), tall.tolist(), deep.tolist()


def swap(piece, axis, start):
    pairs = [(i, i + 1) for i in range(start, lax.axis_size(axis) - 1, 2)]
    return lax.ppermute(piece, axis, pairs + [(j, i) for i, j in pairs])


def per_device(fields, terrain, columns, record_tile, record_cells, record_weights):
    tiles_x, tiles_y = lax.axis_size("gx"), lax.axis_size("gy")
    variables, levels, cells_x, cells_y = fields.shape
    total_x, total_y = cells_x * tiles_x, cells_y * tiles_y
    coarse_x, coarse_y = cells_x // RATIO, cells_y // RATIO
    count = variables * levels
    wide = count * KW
    parents, records = columns.shape[1:]
    entries = record_cells.shape[1]
    scale = 1.0 / np.sqrt(total_x * total_y)
    per = LANES // KW
    f32, b16 = jnp.float32, jnp.bfloat16

    wave_x, wave_y = wave_rows(total_x), wave_rows(total_y)
    by_x = wave_x.reshape(KW, tiles_x, cells_x).transpose(1, 0, 2)
    by_y = wave_y.reshape(KW, tiles_y, cells_y).transpose(1, 0, 2)
    tab_bx = two_parts(by_x, -2)
    tab_byt = two_parts(np.tile(by_y.transpose(0, 2, 1), (1, 1, per)), -1)
    outer, inner = turns(cells_x * np.arange(tiles_x), RATIO * np.arange(coarse_x), total_x)
    tab_a = two_parts(outer, -2)
    tab_c = two_parts(np.pad(inner, ((0, 0), (0, -coarse_x % 16))), -2)
    tab_ay = two_parts(
        np.tile(by_y[:, :, ::RATIO].transpose(0, 2, 1), (1, 1, LANES // coarse_y)), -1
    )
    tab_low_x = two_parts(-4.0 * scale * by_x.transpose(0, 2, 1), -1)
    tab_low_x = np.concatenate([tab_low_x, tab_low_x[..., :KW]], axis=-1)
    tab_low_y = two_parts(np.tile(by_y, (1, per, 1)), -2)
    tab_low_y = np.concatenate(
        [tab_low_y[:, :LANES], tab_low_y[:, :LANES], tab_low_y[:, LANES:]], axis=1
    )

    f = fields.reshape(count, cells_x, cells_y)
    coarse = coarse_x * coarse_y
    padded = -(-coarse // LANES) * LANES
    own = terrain[::RATIO, ::RATIO].astype(f32).reshape(coarse)
    own = jnp.pad(own, (0, padded - coarse)).reshape(padded // LANES, LANES)
    heights = gather(own, "gx").reshape(tiles_x, padded)

    tile, cells = record_tile.T, record_cells.T
    nest, look, xa, xb, ya, yb = call(
        functools.partial(ready_kernel, coarse_y=coarse_y),
        (f, tab_bx, tab_byt, tile, cells, tab_a, tab_c),
        [FAR] * 7,
        [((KW, wide), f32), ((2 * KW, entries * records), b16)] + [((count, cells_y), f32)] * 4,
        [NEAR] * 6,
        [
            pltpu.VMEM(f.shape, f32),
            pltpu.VMEM(tab_bx.shape[1:], b16),
            pltpu.VMEM(tab_byt.shape[1:], b16),
            pltpu.VMEM(tile.shape, jnp.int32),
            pltpu.VMEM(cells.shape, jnp.int32),
            pltpu.VMEM(tab_a.shape, b16),
            pltpu.VMEM(tab_c.shape, b16),
            DMA,
            DMA,
            DMA,
            DMA((4,)),
        ],
    )
    (part,) = call(
        functools.partial(record_kernel, levels=levels, coarse_y=coarse_y, scale=scale),
        (heights, tile, cells, record_weights.T, columns, look, nest, tab_ay),
        [NEAR] * 7 + [FAR],
        [((8, KW // 8 * wide // LANES, LANES), f32)],
        [NEAR],
        [
            pltpu.VMEM((variables, -(-parents // 8) * 8, records), f32),
            pltpu.VMEM((padded, records), f32),
            pltpu.VMEM((count * coarse_y, entries * records), b16),
            pltpu.VMEM((count * coarse_y, entries * records), b16),
            pltpu.VMEM(tab_ay.shape[1:], b16),
            DMA,
        ],
    )
    wide_groups, tall_groups, deep_groups = near_groups(tiles_x, tiles_y)
    pieces = part.reshape(len(wide_groups[0]), -1, LANES)
    mine = jnp.sum(
        lax.all_to_all(pieces, "gx", 0, 0, axis_index_groups=wide_groups, tiled=True).reshape(
            pieces.shape
        ),
        axis=0,
    )
    mine, xa, xb, ya, yb = lax.optimization_barrier((mine, xa, xb, ya, yb))
    xb = swap(xb, "gx", 1)
    mine = jnp.sum(gather(mine, ("gx", "gy"), tall_groups), axis=0)
    mine, xa, xb, ya, yb = lax.optimization_barrier((mine, xa, xb, ya, yb))
    yb, ya = swap(yb, "gy", 1), swap(ya, "gy", 0)
    mine = jnp.sum(gather(mine, "gy", deep_groups), axis=0)
    mine, ya, yb = lax.optimization_barrier((mine, ya, yb))
    mine, xa = lax.optimization_barrier((mine, xa))
    xa = swap(xa, "gx", 0)
    nudge = gather(mine, "gx", wide_groups).reshape(part.shape)

    state, low_x, low_y = call(
        functools.partial(stencil_kernel, variables=variables),
        (mine, f, terrain, xa, xb, ya, yb, tab_low_x, tab_low_y),
        [LOOSE] + [NEAR] * 6 + [FAR] * 2,
        [
            (f.shape, f32),
            (tab_low_x.shape[1:], b16),
            (tab_low_y.shape[1:2] + (per * cells_y,), b16),
        ],
        [NEAR] * 3,
        [pltpu.VMEM(xa.shape, f32)] * 2 + [pltpu.VMEM(tab_low_y.shape[1:], b16), DMA, DMA],
    )
    updated, coeffs = call(
        nudge_kernel,
        (state, nudge, low_x, low_y),
        [NEAR] * 4,
        [(f.shape, f32), ((count, KW, KW), f32)],
        [FAR, FAR],
        [
            pltpu.VMEM(f.shape, f32),
            pltpu.VMEM((count, KW, KW), f32),
            pltpu.VMEM((count // per // 3 * cells_x, per * cells_y), f32),
            DMA((count // per,)),
            DMA,
        ],
    )
    return updated.reshape(fields.shape), coeffs.reshape(variables, levels, KW, KW)


def solution(mesh):
    return jax.shard_map(
        per_device,
        mesh=mesh,
        in_specs=(
            P(None, None, "gx", "gy"),
            P("gx", "gy"),
            P(None, None, ("gx", "gy")),
            P(("gx", "gy"), None),
            P(("gx", "gy"), None),
            P(("gx", "gy"), None),
        ),
        out_specs=(P(None, None, "gx", "gy"), P()),
        check_vma=False,
    )
```

```python
import functools

import jax
import jax.numpy as jnp
import numpy as np
from jax import lax
from jax.experimental import pallas as pl
from jax.experimental.pallas import tpu as pltpu
from jax.sharding import PartitionSpec as P

KW = 32
RATIO = 8
TOP = 12000.0
HIGHEST_CELL = 2999.0
LANES = 128
EXACT = lax.Precision.HIGHEST


def wave_rows(length):
    half = KW // 2
    x = np.arange(length)
    rows = [np.ones(length)]
    for m in range(1, half):
        rows.append(np.sqrt(2.0) * np.cos(2.0 * np.pi * (m * x % length) / length))
    for m in range(half, KW):
        rows.append(np.sqrt(2.0) * np.sin(2.0 * np.pi * ((m - half + 1) * x % length) / length))
    return np.stack(rows)


def turns(outer, inner, length):
    half = KW // 2
    wave = np.arange(KW)
    wave = np.where(wave < half, wave, wave - half + 1)[:, None]
    a = 2.0 * np.pi * (wave * outer[None, :] % length) / length
    c = 2.0 * np.pi * (wave * inner[None, :] % length) / length
    size = np.where(wave == 0, 1.0, np.sqrt(2.0))
    cosine = np.arange(KW)[:, None] < half
    with_cos = size * np.where(cosine, np.cos(a), np.sin(a))
    with_sin = size * np.where(cosine, -np.sin(a), np.cos(a))
    return np.concatenate([with_cos, with_sin]), np.concatenate([np.cos(c), np.sin(c)])


def two_parts(table, axis):
    whole = table.astype(np.float32)
    high = whole.astype(jnp.bfloat16)
    low = (whole - high.astype(np.float32)).astype(jnp.bfloat16)
    return np.concatenate([high, low], axis=axis)


def dot(a, b, dims=((1,), (0,)), precision=None):
    return lax.dot_general(
        a, b, (dims, ((), ())), precision=precision, preferred_element_type=jnp.float32
    )


def rows_lanes(shape):
    return (
        lax.broadcasted_iota(jnp.int32, shape, 0),
        lax.broadcasted_iota(jnp.int32, shape, 1),
    )


def split(x):
    high = x.astype(jnp.bfloat16)
    return high, (x - high.astype(jnp.float32)).astype(jnp.bfloat16)


def by_parity(axis, a, b):
    first = lax.rem(lax.axis_index(axis), 2) == 0
    return jnp.where(first, a, b), jnp.where(first, b, a)


def hot(mask):
    return jnp.where(mask, 1.0, 0.0).astype(jnp.bfloat16)


def ready_kernel(
    f_hbm, bx_hbm, by_hbm, tile_hbm, cells_hbm, taba_hbm, tabc_hbm, p_ref, look_ref,
    xa_ref, xb_ref, ya_ref, yb_ref, f_ref, bx_ref, by_ref, tile_ref, cells_ref, taba_ref, tabc_ref, f_sem, bx_sem, by_sem, small_sem,
    *, coarse_y
):
    count, cells_x, cells_y = f_ref.shape
    per = LANES // KW
    groups = count // per
    fetch = pltpu.make_async_copy(f_hbm, f_ref, f_sem)
    by_copy = pltpu.make_async_copy(by_hbm.at[lax.axis_index("gy")], by_ref, by_sem)
    bx_copy = pltpu.make_async_copy(bx_hbm.at[lax.axis_index("gx")], bx_ref, bx_sem)
    small = [
        pltpu.make_async_copy(a, b, small_sem.at[i])
        for i, (a, b) in enumerate(
            (
                (tile_hbm, tile_ref),
                (cells_hbm, cells_ref),
                (taba_hbm, taba_ref),
                (tabc_hbm, tabc_ref),
            )
        )
    ]
    for copy in (*small, by_copy, fetch, bx_copy):
        copy.start()
    for copy in small:
        copy.wait()
    records = tile_ref.shape[1]
    row_t, _ = rows_lanes((taba_ref.shape[1], records))
    row_c, _ = rows_lanes((tabc_ref.shape[1], records))
    both = dot(taba_ref[...], hot(row_t == tile_ref[...]))
    outer = both[: 2 * KW] + both[2 * KW :]
    cells = cells_ref[...] // coarse_y
    for e in range(cells_ref.shape[0]):
        both = dot(tabc_ref[...], hot(row_c == cells[e : e + 1, :]))
        inner = both[: 2 * KW] + both[2 * KW :]
        turned = outer * inner
        high, low = split(turned[:KW] + turned[KW:])
        look_ref[:KW, e * records : (e + 1) * records] = high
        look_ref[KW:, e * records : (e + 1) * records] = low
    by_copy.wait()
    by4 = by_ref[...].astype(jnp.float32)
    _, lane = rows_lanes(by4.shape)
    spread = jnp.concatenate(
        [
            jnp.where(lane % LANES // KW == q, by4, 0.0).astype(jnp.bfloat16)
            for q in range(per)
        ],
        axis=0,
    )
    fetch.wait()
    bx_copy.wait()
    values = jnp.concatenate(
        [
            jnp.concatenate([f_ref[per * g + q] for q in range(per)], axis=1)
            for g in range(groups)
        ],
        axis=0,
    )
    high, low = split(values)
    both = dot(high, spread)
    along = both[:, :LANES] + both[:, LANES:] + dot(low, spread[:, :LANES])
    high, low = split(
        jnp.concatenate([along[g * cells_x : (g + 1) * cells_x] for g in range(groups)], axis=1)
    )
    both = dot(bx_ref[...], high)
    p_ref[...] = both[:KW] + both[KW:] + dot(bx_ref[:KW, :], low)
    row, lane = rows_lanes((cells_x, cells_y))
    for i in range(count):
        for ref, at in ((xa_ref, cells_x - 1), (xb_ref, 0)):
            ref[i : i + 1, :] = f_ref[i, at : at + 1, :]
        for ref, at in ((ya_ref, cells_y - 1), (yb_ref, 0)):
            edge = jnp.broadcast_to(f_ref[i, :, at : at + 1], (cells_x, cells_y))
            ref[i : i + 1, :] = jnp.sum(jnp.where(row == lane, edge, 0.0), axis=0, keepdims=True)
    for axis, a_ref, b_ref in (("gx", xa_ref, xb_ref), ("gy", ya_ref, yb_ref)):
        a_ref[...], b_ref[...] = by_parity(axis, a_ref[...], b_ref[...])


def reach(k, levels, parents, highest):
    bottoms = [h + (k - 0.5) * (TOP - h) / levels for h in (0.0, highest)]
    tops = [h + (k + 1.5) * (TOP - h) / levels for h in (0.0, highest)]
    step = TOP / parents
    first = int(np.floor((min(bottoms) - 1.0) / step - 0.5))
    last = int(np.ceil((max(tops) + 1.0) / step - 0.5)) + 1
    return max(0, first) // 8 * 8, min(-(-parents // 8), -(-last // 8)) * 8


def record_kernel(
    h_ref, tile_ref, cells_ref, weights_ref, cols_ref, look_ref, p_ref, taby_hbm, d_ref,
    col_ref, pick_ref, high_ref, low_ref, taby_ref, sem, *, levels, coarse_y, scale
):
    variables, parents, records = cols_ref.shape
    tiles, padded = h_ref.shape
    count = variables * levels
    fetch = pltpu.make_async_copy(taby_hbm.at[lax.axis_index("gy")], taby_ref, sem)
    fetch.start()
    tile = tile_ref[...]
    row, _ = rows_lanes((tiles, records))
    tile_hot = hot(row == tile)
    heights = h_ref[...]
    high = jnp.floor(heights * (1.0 / 64.0))
    low = heights - 64.0 * high
    over = ((0,), (0,))
    pick_ref[...] = 64.0 * dot(high.astype(jnp.bfloat16), tile_hot, over) + dot(
        low.astype(jnp.bfloat16), tile_hot, over
    )
    col_ref[...] = jnp.zeros_like(col_ref)
    for v in range(variables):
        col_ref[v, :parents, :] = cols_ref[v].astype(jnp.float32)
    row_c, _ = rows_lanes((padded, records))
    row_b, _ = rows_lanes((coarse_y, records))
    row_p, _ = rows_lanes(col_ref.shape[1:])
    parent = jnp.where(row_p < parents, (row_p.astype(jnp.float32) + 0.5) * (TOP / parents), 1e9)
    cells = cells_ref[...]
    weights = weights_ref[...].astype(jnp.float32)
    for e in range(cells_ref.shape[0]):
        at = slice(e * records, (e + 1) * records)
        cell = cells[e : e + 1, :]
        height = jnp.sum(jnp.where(row_c == cell, pick_ref[...], 0.0), axis=0, keepdims=True)
        in_b = row_b == cell % coarse_y
        inverse = levels / (TOP - height)
        shift_k = height * inverse + 0.5
        apart = parent * inverse - shift_k
        for k in range(levels):
            first, last = reach(k, levels, parents, HIGHEST_CELL)
            hat = jnp.maximum(0.0, 1.0 - jnp.abs(apart[first:last] - float(k)))
            share = weights[e : e + 1, :] / jnp.sum(hat, axis=0, keepdims=True)
            for v in range(variables):
                value = jnp.sum(hat * col_ref[v, first:last, :], axis=0, keepdims=True) * share
                rest = value - value.astype(jnp.bfloat16).astype(jnp.float32)
                i = (v * levels + k) * coarse_y
                high_ref[i : i + coarse_y, at] = jnp.where(in_b, value, 0.0).astype(jnp.bfloat16)
                low_ref[i : i + coarse_y, at] = jnp.where(in_b, rest, 0.0).astype(jnp.bfloat16)
    last = ((1,), (1,))
    both = dot(high_ref[...], look_ref[...], last)
    by_b = both[:, :KW] + both[:, KW:] + dot(low_ref[...], look_ref[:KW, :], last)
    some = LANES // coarse_y
    groups = count // some
    fetch.wait()
    taby = taby_ref[...].astype(jnp.float32)
    tall = jnp.concatenate([taby] * some, axis=0)
    row, lane = rows_lanes(tall.shape)
    width = some * KW
    tall = jnp.where(row // coarse_y == lane % width // KW, tall, 0.0).astype(jnp.bfloat16)
    turned = jnp.concatenate(
        [jnp.transpose(by_b[g * LANES : (g + 1) * LANES]) for g in range(groups)], axis=0
    )
    high, low = split(turned)
    both = dot(high, tall)
    targets = both[:, :width] + both[:, width:] + dot(low, tall[:, :width])
    for g in range(groups):
        target = targets[g * KW : (g + 1) * KW]
        for i in range(some * KW // LANES):
            j = g * (some * KW // LANES) + i
            here = slice(j * LANES, (j + 1) * LANES)
            part = p_ref[:, here] * scale - target[:, i * LANES : (i + 1) * LANES] * (
                RATIO * RATIO * scale
            )
            for m in range(KW // 8):
                d_ref[:, m * p_ref.shape[1] // LANES + j, :] = part[8 * m : 8 * m + 8]


def stencil_kernel(
    after, f_ref, terrain_ref, xb_ref, ya_ref, yb_ref, bx_hbm, by_hbm, out_ref, bx_ref, right_ref, gain_ref,
    east_ref, west_ref, by_ref, bx_sem, by_sem, *, variables
):
    bx_copy = pltpu.make_async_copy(bx_hbm.at[lax.axis_index("gx")], bx_ref, bx_sem)
    by_copy = pltpu.make_async_copy(by_hbm.at[lax.axis_index("gy")], by_ref, by_sem)
    bx_copy.start()
    by_copy.start()
    count, cells_x, cells_y = f_ref.shape
    levels = count // variables
    row, lane = rows_lanes((cells_x, cells_y))
    other = xb_ref[...]
    east_ref[...], west_ref[...] = by_parity("gx", jnp.zeros_like(other), other)
    first = lax.rem(lax.axis_index("gx"), 2) == 0
    for k in range(levels):
        gain_ref[k : k + 1, :] = 0.1 + 0.05 * jnp.where(
            first, -f_ref[k, cells_x - 1 : cells_x, :], f_ref[k, 0:1, :]
        )
    north, south = by_parity("gy", ya_ref[...], yb_ref[...])
    south = jnp.transpose(south)
    north = jnp.transpose(north)
    metric = TOP / (TOP - terrain_ref[...].astype(jnp.float32))
    metric = metric * metric * 0.1
    for i in range(count):
        k = i % levels
        q = f_ref[i]
        wind_x = f_ref[k]
        wind_y = f_ref[levels + k]
        east = jnp.where(row == cells_x - 1, east_ref[i : i + 1, :], pltpu.roll(q, cells_x - 1, 0))
        west = jnp.where(row == 0, west_ref[i : i + 1, :], pltpu.roll(q, 1, 0))
        above = jnp.where(
            lane == cells_y - 1, north[:cells_x, i : i + 1], pltpu.roll(q, cells_y - 1, 1)
        )
        below = jnp.where(lane == 0, south[:cells_x, i : i + 1], pltpu.roll(q, 1, 1))
        transport = wind_x * (east - west) + wind_y * (above - below)
        diffusion = east + west + above + below - 4.0 * q
        upper = f_ref[i + 1] if k < levels - 1 else q
        lower = f_ref[i - 1] if k > 0 else q
        mixing = (upper - 2.0 * q + lower) * metric
        out_ref[i] = q - 0.05 * transport + 0.1 * diffusion + mixing
    by_copy.wait()
    by4 = by_ref[...].astype(jnp.float32)
    block, _ = rows_lanes(by4.shape)
    for q in range(LANES // KW):
        right_ref[:, q * cells_y : (q + 1) * cells_y] = jnp.where(
            block % LANES // KW == q, by4, 0.0
        ).astype(jnp.bfloat16)
    bx_copy.wait()


def nudge_kernel(
    state_ref, n_ref, bx_ref, right_ref, gain_ref, xa_ref, out_hbm, coeffs_hbm, out_ref, coeffs_ref, low_ref, out_sem, coeffs_sem
):
    count, cells_x, cells_y = state_ref.shape
    per = LANES // KW
    groups = count // per
    levels = gain_ref.shape[0]
    edge = lax.rem(lax.axis_index("gx") + 1, 2) * (cells_x - 1)
    nudge = jnp.concatenate(
        [
            jnp.concatenate([n_ref[:, m * groups + g, :] for m in range(KW // 8)], axis=0)
            for g in range(groups)
        ],
        axis=1,
    )
    high, low = split(nudge)
    along = dot(bx_ref[...], jnp.concatenate([high, high, low], axis=0))
    high, low = split(along)
    for i in range(count):
        coeffs_ref[i] = nudge[:, i * KW : (i + 1) * KW]
    copies = [pltpu.make_async_copy(coeffs_ref, coeffs_hbm, coeffs_sem)]
    copies[0].start()
    thirds = 3
    some = groups // thirds
    for third in range(thirds):
        left = jnp.concatenate(
            [
                jnp.concatenate([x[:, g * LANES : (g + 1) * LANES] for x in (high, low, high)], axis=1)
                for g in range(third * some, (third + 1) * some)
            ],
            axis=0,
        )
        low_ref[...] = dot(left, right_ref[...])
        for g in range(some):
            for q in range(per):
                i = per * (third * some + g) + q
                out_ref[i] = state_ref[i] + low_ref[
                    g * cells_x : (g + 1) * cells_x, q * cells_y : (q + 1) * cells_y
                ]
                k = i % levels
                out_ref[i, pl.ds(edge, 1), :] += xa_ref[i : i + 1, :] * gain_ref[k : k + 1, :]
            at = pl.ds(per * (third * some + g), per)
            copies.append(
                pltpu.make_async_copy(out_ref.at[at], out_hbm.at[at], out_sem.at[third * some + g])
            )
            copies[-1].start()
    for copy in copies:
        copy.wait()


FAR = pl.BlockSpec(memory_space=pltpu.HBM)
LOOSE = pl.BlockSpec(memory_space=pl.ANY)
NEAR = pl.BlockSpec(memory_space=pltpu.VMEM)
DMA = pltpu.SemaphoreType.DMA


def call(kernel, ins, specs, outs, out_specs, scratch=()):
    return pl.pallas_call(
        kernel,
        out_shape=[jax.ShapeDtypeStruct(s, d) for s, d in outs],
        in_specs=specs,
        out_specs=out_specs,
        scratch_shapes=list(scratch),
        compiler_params=pltpu.CompilerParams(vmem_limit_bytes=48 << 20),
    )(
        *[
            pltpu.with_memory_space_constraint(x, pltpu.HBM) if spec is FAR else x
            for x, spec in zip(ins, specs)
        ]
    )


def gather(piece, axis, groups=None):
    count = len(groups[0]) if groups else lax.axis_size(axis)
    return lax.all_to_all(
        jnp.broadcast_to(piece[None], (count,) + piece.shape),
        axis, 0, 0, axis_index_groups=groups, tiled=True,
    )


def near_groups(tiles_x, tiles_y):
    every = np.arange(tiles_x * tiles_y).reshape(-1, 4, 2, tiles_y // 2, 2)
    along_gx = np.arange(tiles_x).reshape(-1, 4, 2)
    wide = along_gx.transpose(1, 0, 2).reshape(4, -1)
    tall = every.transpose(0, 2, 3, 1, 4).reshape(-1, 8)
    deep = np.arange(tiles_y).reshape(-1, 2).T
    return wide.tolist(), tall.tolist(), deep.tolist()


def swap(piece, axis, start):
    pairs = [(i, i + 1) for i in range(start, lax.axis_size(axis) - 1, 2)]
    return lax.ppermute(piece, axis, pairs + [(j, i) for i, j in pairs])


def per_device(fields, terrain, columns, record_tile, record_cells, record_weights):
    tiles_x, tiles_y = lax.axis_size("gx"), lax.axis_size("gy")
    variables, levels, cells_x, cells_y = fields.shape
    total_x, total_y = cells_x * tiles_x, cells_y * tiles_y
    coarse_x, coarse_y = cells_x // RATIO, cells_y // RATIO
    count = variables * levels
    wide = count * KW
    parents, records = columns.shape[1:]
    entries = record_cells.shape[1]
    scale = 1.0 / np.sqrt(total_x * total_y)
    per = LANES // KW
    f32, b16 = jnp.float32, jnp.bfloat16

    wave_x, wave_y = wave_rows(total_x), wave_rows(total_y)
    by_x = wave_x.reshape(KW, tiles_x, cells_x).transpose(1, 0, 2)
    by_y = wave_y.reshape(KW, tiles_y, cells_y).transpose(1, 0, 2)
    tab_bx = two_parts(by_x, -2)
    tab_byt = two_parts(np.tile(by_y.transpose(0, 2, 1), (1, 1, per)), -1)
    outer, inner = turns(cells_x * np.arange(tiles_x), RATIO * np.arange(coarse_x), total_x)
    tab_a = two_parts(outer, -2)
    tab_c = two_parts(np.pad(inner, ((0, 0), (0, -coarse_x % 16))), -2)
    tab_ay = two_parts(
        np.tile(by_y[:, :, ::RATIO].transpose(0, 2, 1), (1, 1, LANES // coarse_y)), -1
    )
    tab_low_x = two_parts(-4.0 * scale * by_x.transpose(0, 2, 1), -1)
    tab_low_x = np.concatenate([tab_low_x, tab_low_x[..., :KW]], axis=-1)
    tab_low_y = two_parts(np.tile(by_y, (1, per, 1)), -2)
    tab_low_y = np.concatenate(
        [tab_low_y[:, :LANES], tab_low_y[:, :LANES], tab_low_y[:, LANES:]], axis=1
    )

    f = fields.reshape(count, cells_x, cells_y)
    coarse = coarse_x * coarse_y
    padded = -(-coarse // LANES) * LANES
    own = terrain[::RATIO, ::RATIO].astype(f32).reshape(coarse)
    own = jnp.pad(own, (0, padded - coarse)).reshape(padded // LANES, LANES)
    heights = gather(own, "gx").reshape(tiles_x, padded)

    tile, cells = record_tile.T, record_cells.T
    nest, look, xa, xb, ya, yb = call(
        functools.partial(ready_kernel, coarse_y=coarse_y),
        (f, tab_bx, tab_byt, tile, cells, tab_a, tab_c),
        [FAR] * 7,
        [((KW, wide), f32), ((2 * KW, entries * records), b16)] + [((count, cells_y), f32)] * 4,
        [NEAR] * 6,
        [
            pltpu.VMEM(f.shape, f32),
            pltpu.VMEM(tab_bx.shape[1:], b16),
            pltpu.VMEM(tab_byt.shape[1:], b16),
            pltpu.VMEM(tile.shape, jnp.int32),
            pltpu.VMEM(cells.shape, jnp.int32),
            pltpu.VMEM(tab_a.shape, b16),
            pltpu.VMEM(tab_c.shape, b16),
            DMA,
            DMA,
            DMA,
            DMA((4,)),
        ],
    )
    (part,) = call(
        functools.partial(record_kernel, levels=levels, coarse_y=coarse_y, scale=scale),
        (heights, tile, cells, record_weights.T, columns, look, nest, tab_ay),
        [NEAR] * 7 + [FAR],
        [((8, KW // 8 * wide // LANES, LANES), f32)],
        [NEAR],
        [
            pltpu.VMEM((variables, -(-parents // 8) * 8, records), f32),
            pltpu.VMEM((padded, records), f32),
            pltpu.VMEM((count * coarse_y, entries * records), b16),
            pltpu.VMEM((count * coarse_y, entries * records), b16),
            pltpu.VMEM(tab_ay.shape[1:], b16),
            DMA,
        ],
    )
    wide_groups, tall_groups, deep_groups = near_groups(tiles_x, tiles_y)
    pieces = part.reshape(len(wide_groups[0]), -1, LANES)
    mine = jnp.sum(
        lax.all_to_all(pieces, "gx", 0, 0, axis_index_groups=wide_groups, tiled=True).reshape(
            pieces.shape
        ),
        axis=0,
    )
    mine, xa, xb, ya, yb = lax.optimization_barrier((mine, xa, xb, ya, yb))
    xb = swap(xb, "gx", 1)
    mine = jnp.sum(gather(mine, ("gx", "gy"), tall_groups), axis=0)
    mine, xa, xb, ya, yb = lax.optimization_barrier((mine, xa, xb, ya, yb))
    yb, ya = swap(yb, "gy", 1), swap(ya, "gy", 0)
    mine = jnp.sum(gather(mine, "gy", deep_groups), axis=0)
    mine, ya, yb = lax.optimization_barrier((mine, ya, yb))
    mine, xa = lax.optimization_barrier((mine, xa))
    xa = swap(xa, "gx", 0)
    nudge = gather(mine, "gx", wide_groups).reshape(part.shape)

    state, low_x, low_y, gain = call(
        functools.partial(stencil_kernel, variables=variables),
        (mine, f, terrain, xb, ya, yb, tab_low_x, tab_low_y),
        [LOOSE] + [NEAR] * 5 + [FAR] * 2,
        [
            (f.shape, f32),
            (tab_low_x.shape[1:], b16),
            (tab_low_y.shape[1:2] + (per * cells_y,), b16),
            ((levels, cells_y), f32),
        ],
        [NEAR] * 4,
        [pltpu.VMEM(xb.shape, f32)] * 2 + [pltpu.VMEM(tab_low_y.shape[1:], b16), DMA, DMA],
    )
    updated, coeffs = call(
        nudge_kernel,
        (state, nudge, low_x, low_y, gain, xa),
        [NEAR] * 6,
        [(f.shape, f32), ((count, KW, KW), f32)],
        [FAR, FAR],
        [
            pltpu.VMEM(f.shape, f32),
            pltpu.VMEM((count, KW, KW), f32),
            pltpu.VMEM((count // per // 3 * cells_x, per * cells_y), f32),
            DMA((count // per,)),
            DMA,
        ],
    )
    return updated.reshape(fields.shape), coeffs.reshape(variables, levels, KW, KW)


def solution(mesh):
    return jax.shard_map(
        per_device,
        mesh=mesh,
        in_specs=(
            P(None, None, "gx", "gy"),
            P("gx", "gy"),
            P(None, None, ("gx", "gy")),
            P(("gx", "gy"), None),
            P(("gx", "gy"), None),
            P(("gx", "gy"), None),
        ),
        out_specs=(P(None, None, "gx", "gy"), P()),
        check_vma=False,
    )
```
